32 devices in a mesh: dp: 8 (over y, x, core), tensor: 4 (over z).
Axes of the slice: x: 2, y: 2, z: 4, core: 2. Of those that a mesh axis runs over, the one named last changes fastest.
Arguments:
- x_in: float32 [1024, 1024], P(('dp', 'tensor')), may hold values from -6 to 6
- seq_lengths: int32 [8, 8], P('dp'), may hold values from 1 to 64, 128 in all within a row
- ln1_gain: float32 [2, 1024], P(None, ('dp', 'tensor')), may hold values from 0.5 to 1.5
- ln1_bias: float32 [2, 1024], P(None, ('dp', 'tensor')), may hold values from -3 to 3
- ln2_gain: float32 [2, 1024], P(None, ('dp', 'tensor')), may hold values from 0.5 to 1.5
- ln2_bias: float32 [2, 1024], P(None, ('dp', 'tensor')), may hold values from -3 to 3
- res_bias: float32 [2, 1024], P(None, ('dp', 'tensor')), may hold values from -3 to 3
- w_qkv: bfloat16 [2, 1024, 3, 1024], P(None, 'dp', None, 'tensor'), may hold values from -1 to 1
- b_qkv: float32 [2, 3, 1024], P(None, None, ('tensor', 'dp')), may hold values from -3 to 3
- w_out: bfloat16 [2, 1024, 1024], P(None, 'tensor', 'dp'), may hold values from -0.75 to 0.75
- w_fc: bfloat16 [2, 1024, 4096], P(None, 'dp', 'tensor'), may hold values from -0.1875 to 0.1875
- b_fc: float32 [2, 4096], P(None, ('tensor', 'dp')), may hold values from -3 to 3
- w_proj: bfloat16 [2, 4096, 1024], P(None, 'tensor', 'dp'), may hold values from -0.09375 to 0.09375
- grad_out: float32 [1024, 1024], P(('dp', 'tensor')), may hold values from -6 to 6
Outputs:
- y_out: float32 [1024, 1024], P(('dp', 'tensor'))
- grad_x: float32 [1024, 1024], P(('dp', 'tensor'))
- grad_ln1_gain: float32 [2, 1024], P(None, ('dp', 'tensor'))
- grad_ln1_bias: float32 [2, 1024], P(None, ('dp', 'tensor'))
- grad_ln2_gain: float32 [2, 1024], P(None, ('dp', 'tensor'))
- grad_ln2_bias: float32 [2, 1024], P(None, ('dp', 'tensor'))
- grad_res_bias: float32 [2, 1024], P(None, ('dp', 'tensor'))
- grad_w_qkv: float32 [2, 1024, 3, 1024], P(None, 'dp', None, 'tensor')
- grad_b_qkv: float32 [2, 3, 1024], P(None, None, ('tensor', 'dp'))
- grad_w_out: float32 [2, 1024, 1024], P(None, 'tensor', 'dp')
- grad_w_fc: float32 [2, 1024, 4096], P(None, 'dp', 'tensor')
- grad_b_fc: float32 [2, 4096], P(None, ('tensor', 'dp'))
- grad_w_proj: float32 [2, 4096, 1024], P(None, 'tensor', 'dp')
The draws below stay inside these ranges and needn't reach their ends.
Inputs may be any that keep to these rules, and one draw needn't show every extreme that they name: `seq_lengths`: in every row the lengths sum to 128 and the largest is exactly 64.
All inputs are finite; a program needn't handle non-finite values.
Results may differ from the reference program's by a relative error of at most 0.035.
Values may be sent and summed in bfloat16 or wider, within the bound.
A program may use at most 128 MiB of HBM per device.

```python
import math
import jax
import jax.numpy as jnp
import numpy as np
from jax import lax

D = 1024
HEADS = 16
HD = 64
ROT = 16
FF = 4096
LAYERS = 2
NSEQ = 8
TOK_DEV = 32
GROUP = 128
GROUPS = 8
TOKENS = 1024
MAXLEN = 64
N_DP = 8
N_TENSOR = 4


def draw_w_qkv(key, part):
    fan_scale = D ** (-0.5)
    base_draw = jax.random.truncated_normal(key, -5.0, 5.0, (LAYERS, D, 3, D), jnp.float32) * fan_scale
    return base_draw.astype(jnp.bfloat16)


def spiked(array, rng, source, target, shards_of, factor):
    owner, partner = [(jnp.arange(array.shape[position]) // (array.shape[position] // shards_of)).reshape([-1 if axis == position else 1 for axis in range(array.ndim)]) for position in (source, target)]
    chosen = jax.random.permutation(rng, shards_of)[partner]
    strong = (owner == chosen) | (owner == (partner + shards_of // 2) % shards_of)
    return jnp.where(strong, factor * array, array)


def shard_levels(rng, extent, cuts, least, top_value):
    loudness = 1.0
    for position, parts in cuts:
        heights = jax.random.uniform(jax.random.fold_in(jax.random.fold_in(rng, 6), position), (parts,), jnp.float32, least / len(cuts), top_value / len(cuts))
        loudness = loudness * jnp.repeat(jnp.exp(heights), extent[position] // parts).reshape((-1,) + (1,) * (len(extent) - 1 - position))
    return loudness


def profile(count, total, bound, lean):
    weights = [(1 << 20) // math.isqrt(grade ** lean) + 1 for grade in range(2, count + 1)]
    rest, holding = total - bound - (count - 1), [1] * (count - 1)
    while rest > 0:
        movable = [i for i in range(count - 1) if holding[i] < bound]
        mass, budget = sum([weights[i] for i in movable]), rest
        for i in movable:
            more = min(bound - holding[i], max(1, budget * weights[i] // mass), rest)
            holding[i] = holding[i] + more
            rest = rest - more
    return np.array([bound] + holding)


def ragged(own_key, count, total, limit, lean):
    if count == 2:
        one = jax.random.randint(own_key, (), max(1, total - limit), min(limit, total - 1) + 1)
        return jnp.stack([one, total - one])
    lengths = jnp.asarray(profile(count, total, limit, lean), jnp.int32)
    couples = (count - 1) // 2
    source_of, sink = lengths[1:1 + 2 * couples:2], lengths[2:2 + 2 * couples:2]
    room = jnp.minimum(source_of - 1, limit - sink)
    passed = jax.random.randint(jax.random.fold_in(own_key, 1), (couples,), 0, 1 << 20) % (room + 1)
    lengths = lengths.at[1:1 + 2 * couples:2].set(source_of - passed).at[2:2 + 2 * couples:2].set(sink + passed)
    return lengths[jax.random.permutation(jax.random.fold_in(own_key, 2), count)]


def scatter_about(own_key, dims, scale, limit, pieces=(), kind=jnp.bfloat16):
    loudness = shard_levels(own_key, dims, pieces, -0.22, 0.18) if pieces else 1.0
    entries = jax.random.normal(own_key, dims, jnp.float32) * scale * loudness
    return jnp.minimum(jnp.maximum(entries, -limit), limit).astype(kind)


def bell_draw_with(stream_key, shape, spread, reach, cuts, heavy, kind=jnp.bfloat16):
    result = spread * jax.random.normal(stream_key, shape, jnp.float32)
    if cuts:
        result = result * shard_levels(stream_key, shape, cuts, -0.22, 0.18)
    return jnp.clip(spiked(result, jax.random.fold_in(stream_key, 3), *heavy), -reach, reach).astype(kind)


def setup_inputs(seed: int = 0) -> dict:
    key_of = jax.random.split(jax.random.key(seed), 15)
    return {
        "x_in": scatter_about(key_of[0], (TOKENS, D), 1.0, 6.0, ((0, 32),), jnp.float32),
        "seq_lengths": jax.vmap(lambda own: ragged(own, NSEQ, GROUP, MAXLEN, 2))(jax.random.split(key_of[1], GROUPS)).reshape((GROUPS, NSEQ)).astype(jnp.int32),
        "ln1_gain": jnp.clip(1.0 + 0.1 * jax.random.normal(key_of[2], (LAYERS, D), jnp.float32), 0.5, 1.5),
        "ln1_bias": scatter_about(key_of[3], (LAYERS, D), 0.5, 3.0, ((1, 32),), jnp.float32),
        "ln2_gain": jnp.clip(1.0 + 0.1 * jax.random.normal(key_of[4], (LAYERS, D), jnp.float32), 0.5, 1.5),
        "ln2_bias": scatter_about(key_of[5], (LAYERS, D), 0.5, 3.0, ((1, 32),), jnp.float32),
        "res_bias": scatter_about(key_of[6], (LAYERS, D), 0.5, 3.0, ((1, 32),), jnp.float32),
        "w_qkv": draw_w_qkv(jax.random.fold_in(key_of[14], 71), 0),
        "b_qkv": scatter_about(key_of[8], (LAYERS, 3, D), 0.5, 3.0, ((2, 32),), jnp.float32),
        "w_out": scatter_about(key_of[9], (LAYERS, D, D), (D // 16) ** -0.5, 0.75, ((1, 4), (2, 8))),
        "w_fc": scatter_about(key_of[10], (LAYERS, D, FF), D ** -0.5, 0.1875, ((1, 8), (2, 4))),
        "b_fc": scatter_about(key_of[11], (LAYERS, FF), 0.5, 3.0, ((1, 32),), jnp.float32),
        "w_proj": scatter_about(key_of[12], (LAYERS, FF, D), FF ** -0.5, 0.09375, ((1, 4), (2, 8))),
        "grad_out": bell_draw_with(key_of[13], (TOKENS, D), 1.0, 6.0, ((0, 32),), (0, 1, 32, 2.75), jnp.float32),
    }


EPS = 1e-05
HIGH = lax.Precision.HIGHEST
NEG_FILL = -1e+30

def layer_norm(values, gain_vec, bias_vec):
    average = lax.optimization_barrier(jnp.mean(values, axis=-1, keepdims=True))
    centred = values - average
    variance = lax.optimization_barrier(jnp.mean(centred * centred, axis=-1, keepdims=True))
    return centred * lax.rsqrt(variance + EPS) * gain_vec + bias_vec

def gelu_exact(values):
    return 0.5 * values * (1.0 + jax.scipy.special.erf(values * 0.7071067811865476))

def gelu_slope(values):
    normal_cdf = 0.5 * (1.0 + jax.scipy.special.erf(values * 0.7071067811865476))
    return normal_cdf + values * jnp.exp(-0.5 * values * values) * 0.3989422804014327

def group_layout(seq_len, total_rows):
    ends = jnp.cumsum(seq_len).astype(jnp.int32)
    starts = (ends - seq_len).astype(jnp.int32)
    row_ids = jnp.arange(total_rows, dtype=jnp.int32)
    member = (row_ids[:, None] >= starts[None, :]) & (row_ids[:, None] < ends[None, :])
    seq_index = jnp.arange(seq_len.shape[0], dtype=jnp.int32)
    seq_ids = lax.optimization_barrier(jnp.sum(jnp.where(member, seq_index[None, :], 0), axis=1)).astype(jnp.int32)
    row_start = lax.optimization_barrier(jnp.sum(jnp.where(member, starts[None, :], 0), axis=1)).astype(jnp.int32)
    return (seq_ids, (row_ids - row_start).astype(jnp.int32), row_ids)

def rotary_tables(positions):
    half_rot = ROT // 2
    freq_ids = jnp.arange(half_rot, dtype=jnp.float32)
    inverse = jnp.power(10000.0, -2.0 * freq_ids / ROT)
    angles = positions.astype(jnp.float32)[:, None] * inverse[None, :]
    return (jnp.cos(angles), jnp.sin(angles))

def rotate(vectors, cos_tab, sin_tab, direction_sign):
    half_rot = ROT // 2
    lower_half = vectors[..., :half_rot]
    upper_half = vectors[..., half_rot:ROT]
    cos_b = cos_tab[:, None, :]
    sin_b = sin_tab[:, None, :]
    new_lower = lower_half * cos_b - direction_sign * upper_half * sin_b
    new_upper = upper_half * cos_b + direction_sign * lower_half * sin_b
    return jnp.concatenate([new_lower, new_upper, vectors[..., ROT:]], axis=-1)

def masked_scores(queries, keys, seq_ids, row_ids):
    scores = jnp.einsum('qhd,khd->hqk', queries.astype(jnp.float32), keys.astype(jnp.float32), precision=HIGH) * HD ** (-0.5)
    allowed = (seq_ids[:, None] == seq_ids[None, :]) & (row_ids[None, :] <= row_ids[:, None])
    return jnp.where(allowed[None], scores, NEG_FILL)

def shard_sum(partials):
    rounded = lax.optimization_barrier(partials.astype(jnp.bfloat16))
    return lax.optimization_barrier(jnp.sum(rounded.astype(jnp.float32), axis=0))

def forward_layer(resid, weights, layout):
    gain_one, bias_one, gain_two, bias_two, out_bias, qkv_mat, qkv_vec, out_mat, fc_mat, fc_vec, proj_mat = weights
    seq_ids, row_ids, cos_tab, sin_tab = layout
    row_count = resid.shape[0]
    normed_a = layer_norm(resid, gain_one, bias_one).astype(jnp.bfloat16)
    normed_m = layer_norm(resid, gain_two, bias_two).astype(jnp.bfloat16)
    projected = jnp.dot(normed_a, qkv_mat.reshape(D, 3 * D), preferred_element_type=jnp.float32).reshape(row_count, 3, D) + qkv_vec[None]
    split_heads = projected.reshape(row_count, 3, HEADS, HD)
    queries = rotate(split_heads[:, 0], cos_tab, sin_tab, 1.0).astype(jnp.bfloat16)
    keys = rotate(split_heads[:, 1], cos_tab, sin_tab, 1.0).astype(jnp.bfloat16)
    values = split_heads[:, 2].astype(jnp.bfloat16)
    scores = masked_scores(queries, keys, seq_ids, row_ids)
    top_val = lax.optimization_barrier(jnp.max(scores, axis=-1, keepdims=True))
    exponent_terms = jnp.exp(scores - top_val)
    totals = lax.optimization_barrier(jnp.sum(exponent_terms, axis=-1, keepdims=True))
    attn_probs = (exponent_terms / totals).astype(jnp.bfloat16)
    contexts = jnp.einsum('hqk,khd->qhd', attn_probs.astype(jnp.float32), values.astype(jnp.float32), precision=HIGH).astype(jnp.bfloat16)
    log_totals = (top_val + jnp.log(totals))[..., 0]
    hidden_pre = jnp.dot(normed_m, fc_mat, preferred_element_type=jnp.float32) + fc_vec
    activated = gelu_exact(hidden_pre).astype(jnp.bfloat16)
    partials = jnp.einsum('gtk,tkn->tgn', contexts.reshape(row_count, N_TENSOR, -1).astype(jnp.float32), out_mat.reshape(N_TENSOR, -1, D).astype(jnp.float32), precision=HIGH)
    partials = partials + jnp.einsum('gtk,tkn->tgn', activated.reshape(row_count, N_TENSOR, -1).astype(jnp.float32), proj_mat.reshape(N_TENSOR, -1, D).astype(jnp.float32), precision=HIGH)
    branch = shard_sum(partials)
    new_resid = resid + branch + out_bias
    return (new_resid, (resid, normed_a, normed_m, queries, keys, values, contexts, log_totals, hidden_pre, activated))

def backward_layer(d_resid, saved, weights, layout):
    gain_one, bias_one, gain_two, bias_two, out_bias, qkv_mat, qkv_vec, out_mat, fc_mat, fc_vec, proj_mat = weights
    seq_ids, row_ids, cos_tab, sin_tab = layout
    resid, normed_a, normed_m, queries, keys, values, contexts, log_totals, hidden_pre, activated = saved
    row_count = d_resid.shape[0]
    out_bias_grad = lax.optimization_barrier(jnp.sum(d_resid, axis=0))
    d_rows = d_resid.astype(jnp.bfloat16)
    flat_context = contexts.reshape(row_count, D)
    d_context = jnp.dot(d_rows, out_mat.T, preferred_element_type=jnp.float32).astype(jnp.bfloat16).reshape(row_count, HEADS, HD)
    grad_out_mat = jnp.dot(flat_context.T, d_rows, preferred_element_type=jnp.float32)
    d_act = jnp.dot(d_rows, proj_mat.T, preferred_element_type=jnp.float32)
    grad_proj_mat = jnp.dot(activated.T, d_rows, preferred_element_type=jnp.float32)
    d_pre = d_act * gelu_slope(hidden_pre)
    grad_fc_vec = lax.optimization_barrier(jnp.sum(d_pre, axis=0))
    d_pre_b = d_pre.astype(jnp.bfloat16)
    grad_fc_mat = jnp.dot(normed_m.T, d_pre_b, preferred_element_type=jnp.float32)
    scores = masked_scores(queries, keys, seq_ids, row_ids)
    probs_full = jnp.exp(scores - log_totals[..., None])
    d_probs = jnp.einsum('qhd,khd->hqk', d_context.astype(jnp.float32), values.astype(jnp.float32), precision=HIGH)
    delta = lax.optimization_barrier(jnp.sum(d_context.astype(jnp.float32) * contexts.astype(jnp.float32), axis=-1))
    d_scores = probs_full * (d_probs - jnp.transpose(delta)[:, :, None])
    d_scaled = (d_scores * HD ** (-0.5)).astype(jnp.bfloat16)
    d_queries = jnp.einsum('hqk,khd->qhd', d_scaled.astype(jnp.float32), keys.astype(jnp.float32), precision=HIGH)
    d_keys = jnp.einsum('hqk,qhd->khd', d_scaled.astype(jnp.float32), queries.astype(jnp.float32), precision=HIGH)
    d_values = jnp.einsum('hqk,qhd->khd', probs_full.astype(jnp.bfloat16).astype(jnp.float32), d_context.astype(jnp.float32), precision=HIGH)
    d_queries = rotate(d_queries, cos_tab, sin_tab, -1.0)
    d_keys = rotate(d_keys, cos_tab, sin_tab, -1.0)
    d_projected = jnp.stack([d_queries, d_keys, d_values], axis=1).reshape(row_count, 3, D)
    grad_qkv_vec = lax.optimization_barrier(jnp.sum(d_projected, axis=0))
    d_projected_b = d_projected.astype(jnp.bfloat16)
    grad_qkv_mat = jnp.dot(normed_a.T, d_projected_b.reshape(row_count, 3 * D), preferred_element_type=jnp.float32).reshape(D, 3, D)
    d_norm_a = shard_sum(jnp.einsum('gctk,dctk->tgd', d_projected_b.reshape(row_count, 3, N_TENSOR, -1).astype(jnp.float32), qkv_mat.reshape(D, 3, N_TENSOR, -1).astype(jnp.float32), precision=HIGH))
    d_norm_m = shard_sum(jnp.einsum('gtk,dtk->tgd', d_pre_b.reshape(row_count, N_TENSOR, -1).astype(jnp.float32), fc_mat.reshape(D, N_TENSOR, -1).astype(jnp.float32), precision=HIGH))
    unused_one, back_one = jax.vjp(layer_norm, resid, gain_one, bias_one)
    d_res_one, grad_gain_one, grad_bias_one = back_one(d_norm_a)
    unused_two, back_two = jax.vjp(layer_norm, resid, gain_two, bias_two)
    d_res_two, grad_gain_two, grad_bias_two = back_two(d_norm_m)
    d_input = d_resid + d_res_one + d_res_two
    return (d_input, (grad_gain_one, grad_bias_one, grad_gain_two, grad_bias_two, out_bias_grad, grad_qkv_mat, grad_qkv_vec, grad_out_mat, grad_fc_mat, grad_fc_vec, grad_proj_mat))

def reference(x_in, seq_lengths, ln1_gain, ln1_bias, ln2_gain, ln2_bias, res_bias, w_qkv, b_qkv, w_out, w_fc, b_fc, w_proj, grad_out):
    group_rows = TOK_DEV * N_TENSOR
    params = (ln1_gain, ln1_bias, ln2_gain, ln2_bias, res_bias, w_qkv, b_qkv, w_out, w_fc, b_fc, w_proj)
    x_groups = x_in.reshape(N_DP, group_rows, D)
    d_groups = grad_out.reshape(N_DP, group_rows, D)

    def per_group(carry, inputs):
        x_grp, len_grp, d_grp = inputs
        seq_ids, positions, row_ids = group_layout(len_grp, group_rows)
        cos_tab, sin_tab = rotary_tables(positions)
        layout = (seq_ids, row_ids, cos_tab, sin_tab)
        resid = x_grp
        saved_all = []
        for layer_idx in range(LAYERS):
            weights = tuple((param_arr[layer_idx] for param_arr in params))
            resid, saved = forward_layer(resid, weights, layout)
            saved_all.append(saved)
        d_resid = d_grp
        layer_grads = [None] * LAYERS
        for layer_idx in reversed(range(LAYERS)):
            weights = tuple((param_arr[layer_idx] for param_arr in params))
            d_resid, layer_grads[layer_idx] = backward_layer(d_resid, saved_all[layer_idx], weights, layout)
        new_carry = tuple((carry[member_idx] + jnp.stack([layer_grads[layer_idx][member_idx] for layer_idx in range(LAYERS)]) for member_idx in range(len(params))))
        return (new_carry, (resid, d_resid))
    init = tuple((jnp.zeros(param_arr.shape, jnp.float32) for param_arr in params))
    totals, outputs = lax.scan(per_group, init, (x_groups, seq_lengths, d_groups))
    y_groups, dx_groups = outputs
    g_ln1_gain, g_ln1_bias, g_ln2_gain, g_ln2_bias, g_res_bias, g_w_qkv, g_b_qkv, g_w_out, g_w_fc, g_b_fc, g_w_proj = totals
    return (y_groups.reshape(-1, D), dx_groups.reshape(-1, D), g_ln1_gain, g_ln1_bias, g_ln2_gain, g_ln2_bias, g_res_bias, g_w_qkv, g_b_qkv, g_w_out, g_w_fc, g_b_fc, g_w_proj)
```

```python
import functools

import jax
import jax.numpy as jnp
from jax import lax
from jax.experimental import pallas as pl
from jax.experimental.pallas import tpu as pltpu
from jax.sharding import PartitionSpec as P

HD = 64
ROT = 16


EPS = 1e-05
NEG_FILL = -1e30


def gelu_exact(values):
    return 0.5 * values * (1.0 + jax.scipy.special.erf(values * 0.7071067811865476))


def gelu_slope(values):
    normal_cdf = 0.5 * (1.0 + jax.scipy.special.erf(values * 0.7071067811865476))
    return normal_cdf + values * jnp.exp(-0.5 * values * values) * 0.3989422804014327


def group_layout(seq_len, total_rows):
    ends = jnp.cumsum(seq_len)
    starts = ends - seq_len
    row_ids = jnp.arange(total_rows, dtype=jnp.int32)
    member = (row_ids[:, None] >= starts[None, :]) & (row_ids[:, None] < ends[None, :])
    seq_index = jnp.arange(seq_len.shape[0], dtype=jnp.int32)
    seq_ids = jnp.sum(jnp.where(member, seq_index[None, :], 0), axis=1)
    row_start = jnp.sum(jnp.where(member, starts[None, :], 0), axis=1)
    return (seq_ids, row_ids - row_start, row_ids)


def rotary_tables(positions):
    half_rot = ROT // 2
    freq_ids = jnp.arange(half_rot, dtype=jnp.float32)
    inverse = jnp.power(10000.0, -2.0 * freq_ids / ROT)
    angles = positions.astype(jnp.float32)[:, None] * inverse[None, :]
    return (jnp.cos(angles), jnp.sin(angles))


def rotate(vectors, cos_tab, sin_tab, direction_sign):
    half_rot = ROT // 2
    lower_half = vectors[..., :half_rot]
    upper_half = vectors[..., half_rot:ROT]
    cos_b = cos_tab[:, None, :]
    sin_b = sin_tab[:, None, :]
    new_lower = lower_half * cos_b - direction_sign * upper_half * sin_b
    new_upper = upper_half * cos_b + direction_sign * lower_half * sin_b
    return jnp.concatenate([new_lower, new_upper, vectors[..., ROT:]], axis=-1)


def masked_block(q_blk, keys, q_seq, q_row, seq_ids, row_ids):
    scores = jnp.einsum("qhd,khd->hqk", q_blk, keys, preferred_element_type=jnp.float32) * HD ** (
        -0.5
    )
    allowed = (q_seq[:, None] == seq_ids[None, :]) & (row_ids[None, :] <= q_row[:, None])
    return jnp.where(allowed[None], scores, NEG_FILL)


def attention_forward(queries, keys, values, seq_ids, row_ids):
    total_rows, heads_here, head_dim = queries.shape
    block_rows = min(512, total_rows)
    blocks = total_rows // block_rows

    def one_block(inputs):
        q_blk, q_seq, q_row = inputs
        scores = masked_block(q_blk, keys, q_seq, q_row, seq_ids, row_ids)
        top_val = jnp.max(scores, axis=-1, keepdims=True)
        exponent_terms = jnp.exp(scores - top_val)
        totals = jnp.sum(exponent_terms, axis=-1, keepdims=True)
        attn_probs = (exponent_terms / totals).astype(jnp.bfloat16)
        context = jnp.einsum(
            "hqk,khd->qhd", attn_probs, values, preferred_element_type=jnp.float32
        ).astype(jnp.bfloat16)
        return (context, (top_val + jnp.log(totals))[..., 0])

    contexts, log_totals = lax.map(
        one_block,
        (
            queries.reshape(blocks, block_rows, heads_here, head_dim),
            seq_ids.reshape(blocks, block_rows),
            row_ids.reshape(blocks, block_rows),
        ),
    )
    return (contexts.reshape(total_rows, heads_here, head_dim), log_totals)


def attention_backward(queries, keys, values, contexts, d_context, log_totals, seq_ids, row_ids):
    total_rows, heads_here, head_dim = queries.shape
    block_rows = min(512, total_rows)
    blocks = total_rows // block_rows

    def one_block(carry, inputs):
        d_keys, d_values = carry
        q_blk, c_blk, dc_blk, lse_blk, q_seq, q_row = inputs
        scores = masked_block(q_blk, keys, q_seq, q_row, seq_ids, row_ids)
        probs_full = jnp.exp(scores - lse_blk[..., None])
        d_probs = jnp.einsum("qhd,khd->hqk", dc_blk, values, preferred_element_type=jnp.float32)
        delta = jnp.sum(dc_blk.astype(jnp.float32) * c_blk.astype(jnp.float32), axis=-1)
        d_scores = probs_full * (d_probs - jnp.transpose(delta)[:, :, None])
        d_scaled = (d_scores * HD ** (-0.5)).astype(jnp.bfloat16)
        d_q = jnp.einsum("hqk,khd->qhd", d_scaled, keys, preferred_element_type=jnp.float32)
        d_keys = d_keys + jnp.einsum(
            "hqk,qhd->khd", d_scaled, q_blk, preferred_element_type=jnp.float32
        )
        d_values = d_values + jnp.einsum(
            "hqk,qhd->khd",
            probs_full.astype(jnp.bfloat16),
            dc_blk,
            preferred_element_type=jnp.float32,
        )
        return ((d_keys, d_values), d_q)

    zero_keys = jnp.zeros(keys.shape, jnp.float32)
    shape_blk = (blocks, block_rows, heads_here, head_dim)
    carry_out, d_queries = lax.scan(
        one_block,
        (zero_keys, zero_keys),
        (
            queries.reshape(shape_blk),
            contexts.reshape(shape_blk),
            d_context.reshape(shape_blk),
            log_totals,
            seq_ids.reshape(blocks, block_rows),
            row_ids.reshape(blocks, block_rows),
        ),
    )
    return (d_queries.reshape(total_rows, heads_here, head_dim), carry_out[0], carry_out[1])


MESH = pl.DeviceIdType.MESH
ANY = pl.BlockSpec(memory_space=pl.ANY)
VMEM = pl.BlockSpec(memory_space=pltpu.VMEM)
N_SEMS = 160
N_LOCAL = 32


class Links:
    def __init__(self, n_dp, n_tensor, send_sems, recv_sems, local_sems):
        self.n_dp, self.n_tensor = n_dp, n_tensor
        self.dp, self.tensor = lax.axis_index("dp"), lax.axis_index("tensor")
        self.send_sems, self.recv_sems, self.local_sems = send_sems, recv_sems, local_sems
        self.used, self.used_local = 0, 0
        self.sent = []

    def send(self, src, dst, **where):
        copy = pltpu.make_async_remote_copy(
            src_ref=src,
            dst_ref=dst,
            send_sem=self.send_sems.at[self.used],
            recv_sem=self.recv_sems.at[self.used],
            device_id=where,
            device_id_type=MESH,
        )
        self.used += 1
        copy.start()
        self.sent.append(copy)
        return copy

    def local(self, src, dst):
        copy = pltpu.make_async_copy(src, dst, self.local_sems.at[self.used_local])
        self.used_local += 1
        copy.start()
        return copy

    def dp_peer(self, step):
        return lax.rem(self.dp + step, self.n_dp)

    def tensor_peer(self, step):
        return lax.rem(self.tensor + step, self.n_tensor)

    def tensor_from(self, step):
        return lax.rem(self.tensor + self.n_tensor - step, self.n_tensor)

    def barrier(self, with_dp):
        sem = pltpu.get_barrier_semaphore()
        count = self.n_tensor - 1
        for step in range(1, self.n_tensor):
            pl.semaphore_signal(
                sem, inc=1, device_id={"tensor": self.tensor_peer(step)}, device_id_type=MESH
            )
        if with_dp:
            count += self.n_dp - 1
            for step in range(1, self.n_dp):
                pl.semaphore_signal(
                    sem, inc=1, device_id={"dp": self.dp_peer(step)}, device_id_type=MESH
                )
        pl.semaphore_wait(sem, count)

    def finish(self):
        for copy in self.sent:
            copy.wait_send()


def start_dp_gather(links, items):
    chips = links.n_dp // 2
    core, chip = lax.rem(links.dp, 2), links.dp // 2
    partner = links.dp + 1 - 2 * core
    direct = []
    for step in range(1, chips):
        peer = lax.rem(chip + step, chips) * 2 + core
        for own, slot in items:
            direct.append(links.send(own, slot(links.dp), dp=peer))
    passed = [links.send(own, slot(links.dp), dp=partner) for own, slot in items]
    return direct, passed


def end_dp_gather(links, items, direct, passed):
    chips = links.n_dp // 2
    core, chip = lax.rem(links.dp, 2), links.dp // 2
    partner = links.dp + 1 - 2 * core
    position = 0
    for step in range(1, chips):
        origin = lax.rem(chip + chips - step, chips) * 2 + core
        for _, slot in items:
            direct[position].wait_recv()
            position += 1
            passed.append(links.send(slot(origin), slot(origin), dp=partner))
    for copy in passed:
        copy.wait_recv()


def row_slot(ref, rows):
    return lambda d: ref.at[pl.ds(pl.multiple_of(d * rows, rows), rows)]


def weight_slot(ref, layer, axis, size):
    if axis is None:
        return lambda d: ref.at[d, layer]
    if axis == 0:
        return lambda d: ref.at[layer, pl.ds(pl.multiple_of(d * size, size), size), :]
    return lambda d: ref.at[layer, :, pl.ds(pl.multiple_of(d * size, size), size)]


def scratch_sems():
    return [
        pltpu.SemaphoreType.DMA((N_SEMS,)),
        pltpu.SemaphoreType.DMA((N_SEMS,)),
        pltpu.SemaphoreType.DMA((N_LOCAL,)),
    ]


def entry_kernel(n_dp, n_tensor, axes, *refs):
    n_w = len(axes)
    w_in, (small_in, rows_in) = refs[:n_w], refs[n_w : n_w + 2]
    w_out = refs[n_w + 2 : 2 * n_w + 2]
    small_out, rows_out = refs[2 * n_w + 2 : 2 * n_w + 4]
    held = refs[2 * n_w + 4 : 3 * n_w + 4]
    links = Links(n_dp, n_tensor, *refs[3 * n_w + 4 :])
    loads = [links.local(src, dst) for src, dst in zip(w_in, held)]
    links.barrier(True)
    layers = w_in[0].shape[0]
    small_own = links.local(small_in, small_out.at[links.tensor, links.dp])
    row_count = rows_in.shape[0]
    slot = row_slot(rows_out, row_count)
    rows_own = links.local(rows_in, slot(links.tensor))
    rows_sent = [
        links.send(rows_in, slot(links.tensor), tensor=links.tensor_peer(step))
        for step in range(1, n_tensor)
    ]
    small_sent = [
        links.send(small_in, small_out.at[links.tensor, links.dp], dp=links.dp_peer(step))
        for step in range(1, n_dp)
    ]
    for copy in loads:
        copy.wait()
    items = []
    for layer in range(layers):
        for index, axis in enumerate(axes):
            size = w_in[index].shape[1 + axis] if axis is not None else 0
            items.append(
                (held[index].at[layer], weight_slot(w_out[index], layer, axis, size))
            )
    direct, passed = start_dp_gather(links, items)
    own = [links.local(src, slot_of(links.dp)) for src, slot_of in items]
    small_own.wait()
    for copy in small_sent:
        copy.wait_recv()
    small_wide = [
        links.send(
            small_out.at[links.tensor], small_out.at[links.tensor], tensor=links.tensor_peer(step)
        )
        for step in range(1, n_tensor)
    ]
    end_dp_gather(links, items, direct, passed)
    for copy in rows_sent + small_wide:
        copy.wait_recv()
    rows_own.wait()
    for copy in own:
        copy.wait()
    links.finish()


def start_scatter(links, part, landing):
    rows = landing.shape[1]
    return [
        links.send(
            row_slot(part, rows)(links.tensor_peer(step)),
            landing.at[step - 1],
            tensor=links.tensor_peer(step),
        )
        for step in range(1, links.n_tensor)
    ]


def end_scatter(links, part, landing, copies):
    rows = landing.shape[1]
    total = part[pl.ds(pl.multiple_of(links.tensor * rows, rows), rows), :].astype(jnp.float32)
    for step, copy in enumerate(copies):
        copy.wait_recv()
        total = total + landing[step].astype(jnp.float32)
    return total


def start_gather(links, out, own):
    rows = own.shape[0]
    slot = row_slot(out, rows)
    copies = [
        links.send(own, slot(links.tensor), tensor=links.tensor_peer(step))
        for step in range(1, links.n_tensor)
    ]
    return copies, links.local(own, slot(links.tensor))


def unit_rows(values):
    average = jnp.mean(values, axis=-1, keepdims=True)
    centred = values - average
    variance = jnp.mean(centred * centred, axis=-1, keepdims=True)
    scale = lax.rsqrt(variance + EPS)
    return centred * scale, scale


def back_unit(values, grad):
    unit, scale = unit_rows(values)
    return scale * (
        grad
        - jnp.mean(grad, axis=-1, keepdims=True)
        - unit * jnp.mean(grad * unit, axis=-1, keepdims=True)
    )


def forward_kernel(n_dp, n_tensor, part, resid, bias, new_resid, rows_out, landing, own, *sems):
    links = Links(n_dp, n_tensor, *sems)
    links.barrier(False)
    branch = end_scatter(links, part, landing, start_scatter(links, part, landing))
    values = resid[...] + branch + bias[...]
    new_resid[...] = values
    own[...] = unit_rows(values)[0].astype(jnp.bfloat16)
    copies, local = start_gather(links, rows_out, own)
    for copy in copies:
        copy.wait_recv()
    local.wait()
    links.finish()


def backward_kernel(
    n_dp, n_tensor, part_y, part_e, resid, bias, dres, y_out, d_out, rows_out, land_y, land_e, own, *sems
):
    links = Links(n_dp, n_tensor, *sems)
    links.barrier(False)
    copies_e = start_scatter(links, part_e, land_e)
    copies_y = start_scatter(links, part_y, land_y) if part_y is not None else None
    grad = end_scatter(links, part_e, land_e, copies_e)
    values = resid[...]
    new_d = dres[...] + back_unit(values, grad)
    d_out[...] = new_d
    own[...] = new_d.astype(jnp.bfloat16)
    copies, local = start_gather(links, rows_out, own)
    if part_y is not None:
        y_out[...] = values + end_scatter(links, part_y, land_y, copies_y) + bias[...]
    for copy in copies:
        copy.wait_recv()
    local.wait()
    links.finish()


def exit_kernel(n_dp, n_tensor, n_act, *refs):
    acts, refs = refs[:n_act], refs[n_act:]
    cross, small, part_e, resid, dres = refs[:5]
    act_out, refs = refs[5 : 5 + n_act], refs[5 + n_act :]
    cross_out, small_out, d_out = refs[:3]
    held, refs = refs[3 : 3 + n_act], refs[3 + n_act :]
    land_e, land_s, half_s, land_t = refs[:4]
    links = Links(n_dp, n_tensor, *refs[4:])
    loads = [links.local(src, dst) for src, dst in zip(acts, held)]
    links.barrier(True)
    copies_e = start_scatter(links, part_e, land_e)
    small_sent = [
        links.send(small.at[links.dp_peer(step)], land_s.at[step - 1], dp=links.dp_peer(step))
        for step in range(1, n_dp)
    ]
    for copy in loads:
        copy.wait()
    items = [
        (own, row_slot(ref, own.shape[0])) for own, ref in zip(held, act_out)
    ]
    direct, passed = start_dp_gather(links, items)
    cross_sent = [
        links.send(cross.at[links.dp_peer(step)], cross_out.at[links.dp], dp=links.dp_peer(step))
        for step in range(1, n_dp)
    ]
    own = [links.local(src, slot_of(links.dp)) for src, slot_of in items]
    own.append(links.local(cross.at[links.dp], cross_out.at[links.dp]))
    total = small[links.dp]
    for step, copy in enumerate(small_sent):
        copy.wait_recv()
        total = total + land_s[step]
    half_s[...] = total
    wide = [
        links.send(half_s, land_t.at[step - 1], tensor=links.tensor_peer(step))
        for step in range(1, n_tensor)
    ]
    grad = end_scatter(links, part_e, land_e, copies_e)
    d_out[...] = dres[...] + back_unit(resid[...], grad)
    for step, copy in enumerate(wide):
        copy.wait_recv()
        total = total + land_t[step]
    small_out[...] = total
    end_dp_gather(links, items, direct, passed)
    for copy in cross_sent:
        copy.wait_recv()
    for copy in own:
        copy.wait()
    links.finish()


def call(kernel, name, collective, outs, out_specs, in_specs, scratch, args):
    return pl.pallas_call(
        kernel,
        out_shape=outs,
        in_specs=in_specs,
        out_specs=out_specs,
        scratch_shapes=scratch + scratch_sems(),
        name=name,
        compiler_params=pltpu.CompilerParams(
            collective_id=collective, has_side_effects=True, vmem_limit_bytes=40 << 20
        ),
    )(*args)


def shaped(shape, dtype):
    return jax.ShapeDtypeStruct(tuple(shape), dtype)


def pack_rows(parts):
    flat = jnp.concatenate([part.reshape(-1) for part in parts])
    padded = -(-flat.shape[0] // 1024) * 1024
    return jnp.pad(flat, (0, padded - flat.shape[0])).reshape(-1, 128)


def per_device(
    x_in,
    seq_lengths,
    ln1_gain,
    ln1_bias,
    ln2_gain,
    ln2_bias,
    res_bias,
    w_qkv,
    b_qkv,
    w_out,
    w_fc,
    b_fc,
    w_proj,
    grad_out,
):
    n_tensor, n_dp = lax.axis_size("tensor"), lax.axis_size("dp")
    my_tensor = lax.axis_index("tensor")
    bf16, f32 = jnp.bfloat16, jnp.float32
    my_rows, width = x_in.shape
    group_rows = my_rows * n_tensor
    total_rows = group_rows * n_dp
    layer_count = w_qkv.shape[0]
    heads_here = w_qkv.shape[3] // HD
    dp_width = width // n_dp
    vec_width = dp_width // n_tensor

    columns_ok = dp_width % 128 == 0
    shards = (w_qkv.reshape(layer_count, dp_width, -1), w_out, w_fc, w_proj)
    axes = (0, 1 if columns_ok else None, 0, 1 if columns_ok else None)
    gathered = []
    for shard, axis in zip(shards, axes):
        shape = list(shard.shape)
        if axis is None:
            shape = [n_dp] + shape
        else:
            shape[1 + axis] *= n_dp
        gathered.append(shaped(shape, bf16))
    smalls = (
        jnp.stack([ln1_gain, ln1_bias, ln2_gain, ln2_bias, res_bias]),
        b_qkv,
        b_fc,
    )
    packed = pack_rows(smalls)
    unit_first = unit_rows(x_in)[0].astype(bf16)
    rows_first = jnp.concatenate([unit_first, grad_out.astype(bf16)], axis=1)
    entry = call(
        functools.partial(entry_kernel, n_dp, n_tensor, axes),
        "entry",
        0,
        tuple(gathered)
        + (
            shaped((n_tensor, n_dp) + packed.shape, f32),
            shaped((group_rows, 2 * width), bf16),
        ),
        (ANY,) * 4 + (VMEM, VMEM),
        [ANY] * 4 + [VMEM, VMEM],
        [pltpu.VMEM(shard.shape, bf16) for shard in shards],
        shards + (packed, rows_first),
    )
    qkv_all, out_all, fc_all, proj_all, small_all, rows_all = entry
    if not columns_ok:
        out_all = jnp.transpose(out_all, (1, 2, 0, 3)).reshape(layer_count, -1, width)
        proj_all = jnp.transpose(proj_all, (1, 2, 0, 3)).reshape(layer_count, -1, width)
    small_all = small_all.reshape(n_tensor, n_dp, -1)
    n_gain = smalls[0].size
    vectors = jnp.transpose(
        small_all[:, :, :n_gain].reshape(n_tensor, n_dp, 5, layer_count, vec_width),
        (2, 3, 1, 0, 4),
    ).reshape(5, layer_count, width)
    gain_one, bias_one, gain_two, bias_two, out_bias = vectors
    mine = lax.dynamic_index_in_dim(small_all, my_tensor, 0, keepdims=False)
    qkv_vecs = jnp.transpose(
        mine[:, n_gain : n_gain + b_qkv.size].reshape((n_dp,) + b_qkv.shape), (1, 2, 0, 3)
    ).reshape(layer_count, 1, -1)
    fc_vecs = jnp.transpose(
        mine[:, n_gain + b_qkv.size : n_gain + b_qkv.size + b_fc.size].reshape(
            (n_dp,) + b_fc.shape
        ),
        (1, 0, 2),
    ).reshape(layer_count, 1, -1)

    seq_ids, positions, row_ids = group_layout(seq_lengths[0], group_rows)
    cos_tab, sin_tab = rotary_tables(positions)
    unit_full, d_rows = rows_all[:, :width], rows_all[:, width:]
    resid = x_in
    saved = []
    for layer in range(layer_count):
        unit_wide = unit_full.astype(f32)
        normed_a = (unit_wide * gain_one[layer] + bias_one[layer]).astype(bf16)
        normed_m = (unit_wide * gain_two[layer] + bias_two[layer]).astype(bf16)
        projected = (
            jnp.dot(normed_a, qkv_all[layer], preferred_element_type=f32) + qkv_vecs[layer]
        )
        split_heads = projected.reshape(group_rows, 3, heads_here, HD)
        queries = rotate(split_heads[:, 0], cos_tab, sin_tab, 1.0).astype(bf16)
        keys = rotate(split_heads[:, 1], cos_tab, sin_tab, 1.0).astype(bf16)
        values = split_heads[:, 2].astype(bf16)
        contexts, log_totals = attention_forward(queries, keys, values, seq_ids, row_ids)
        hidden_pre = jnp.dot(normed_m, fc_all[layer], preferred_element_type=f32) + fc_vecs[layer]
        activated = gelu_exact(hidden_pre).astype(bf16)
        flat_context = contexts.reshape(group_rows, -1)
        partial = (
            jnp.dot(flat_context, out_all[layer], preferred_element_type=f32)
            + jnp.dot(activated, proj_all[layer], preferred_element_type=f32)
        ).astype(bf16)
        saved.append(
            (resid, unit_full, queries, keys, values, contexts, log_totals, hidden_pre, activated)
        )
        if layer + 1 < layer_count:
            resid, unit_full = call(
                functools.partial(forward_kernel, n_dp, n_tensor),
                f"forward{layer}",
                1 + layer,
                (shaped(x_in.shape, f32), shaped((group_rows, width), bf16)),
                (VMEM, VMEM),
                [VMEM] * 3,
                [
                    pltpu.VMEM((n_tensor - 1, my_rows, width), bf16),
                    pltpu.VMEM((my_rows, width), bf16),
                ],
                (partial, resid, out_bias[layer][None]),
            )
    d_resid = grad_out
    acts, cross, sums = [None] * layer_count, [None] * layer_count, [None] * layer_count
    y_out = None
    for layer in reversed(range(layer_count)):
        (
            layer_input,
            unit_full,
            queries,
            keys,
            values,
            contexts,
            log_totals,
            hidden_pre,
            activated,
        ) = saved[layer]
        out_bias_grad = jnp.sum(d_resid, axis=0)
        flat_context = contexts.reshape(group_rows, -1)
        transposed = (((1,), (1,)), ((), ()))
        d_context = lax.dot_general(
            d_rows, out_all[layer], transposed, preferred_element_type=f32
        ).astype(bf16)
        d_act = lax.dot_general(d_rows, proj_all[layer], transposed, preferred_element_type=f32)
        d_pre_b = (d_act * gelu_slope(hidden_pre)).astype(bf16)
        d_queries, d_keys, d_values = attention_backward(
            queries,
            keys,
            values,
            contexts,
            d_context.reshape(group_rows, heads_here, HD),
            log_totals,
            seq_ids,
            row_ids,
        )
        d_queries = rotate(d_queries, cos_tab, sin_tab, -1.0)
        d_keys = rotate(d_keys, cos_tab, sin_tab, -1.0)
        flat_dqkv = (
            jnp.stack([d_queries, d_keys, d_values], axis=1).reshape(group_rows, -1).astype(bf16)
        )
        d_a = lax.dot_general(flat_dqkv, qkv_all[layer], transposed, preferred_element_type=f32)
        d_m = lax.dot_general(d_pre_b, fc_all[layer], transposed, preferred_element_type=f32)
        unit_wide = unit_full.astype(f32)
        sums[layer] = (
            jnp.sum(d_a * unit_wide, axis=0),
            jnp.sum(d_a, axis=0),
            jnp.sum(d_m * unit_wide, axis=0),
            jnp.sum(d_m, axis=0),
            out_bias_grad,
        )
        part_e = (d_a * gain_one[layer] + d_m * gain_two[layer]).astype(bf16)
        acts[layer] = (flat_context, activated, flat_dqkv, d_pre_b)
        cross[layer] = jnp.stack([unit_full, d_rows]).reshape(2, group_rows, n_dp, dp_width)
        land = pltpu.VMEM((n_tensor - 1, my_rows, width), bf16)
        if layer > 0:
            last = layer + 1 == layer_count
            d_shape = shaped(x_in.shape, f32)
            rows_shape = shaped((group_rows, width), bf16)
            own = pltpu.VMEM((my_rows, width), bf16)
            if last:
                y_out, d_resid, d_rows = call(
                    functools.partial(backward_kernel, n_dp, n_tensor),
                    f"backward{layer}",
                    layer_count + layer,
                    (d_shape, d_shape, rows_shape),
                    (VMEM,) * 3,
                    [VMEM] * 5,
                    [land, land, own],
                    (partial, part_e, layer_input, out_bias[layer][None], d_resid),
                )
            else:

                def no_y(e, r, d, d_o, r_o, l_e, o, *sems):
                    backward_kernel(
                        n_dp, n_tensor, None, e, r, None, d, None, d_o, r_o, None, l_e, o, *sems
                    )

                d_resid, d_rows = call(
                    no_y,
                    f"backward{layer}",
                    layer_count + layer,
                    (d_shape, rows_shape),
                    (VMEM,) * 2,
                    [VMEM] * 3,
                    [land, own],
                    (part_e, layer_input, d_resid),
                )
    flat_acts = [array for group in acts for array in group]
    n_act = len(flat_acts)
    cross_in = jnp.transpose(jnp.stack(cross), (3, 0, 1, 2, 4))
    stacked = jnp.stack([jnp.stack(group) for group in sums]).reshape(-1, width)
    n_sums = stacked.shape[0]
    padded = -(-n_sums // 8) * 8
    small_in = jnp.transpose(
        jnp.pad(stacked, ((0, padded - n_sums), (0, 0))).reshape(padded, n_dp, dp_width), (1, 0, 2)
    )
    small_block = (padded, dp_width)
    results = call(
        functools.partial(exit_kernel, n_dp, n_tensor, n_act),
        "exit",
        2 * layer_count,
        tuple(shaped((total_rows, array.shape[1]), bf16) for array in flat_acts)
        + (shaped(cross_in.shape, bf16), shaped(small_block, f32), shaped(x_in.shape, f32)),
        (ANY,) * n_act + (VMEM,) * 3,
        [ANY] * n_act + [VMEM] * 5,
        [pltpu.VMEM(array.shape, bf16) for array in flat_acts]
        + [
            land,
            pltpu.VMEM((n_dp - 1,) + small_block, f32),
            pltpu.VMEM(small_block, f32),
            pltpu.VMEM((n_tensor - 1,) + small_block, f32),
        ],
        tuple(flat_acts) + (cross_in, small_in, part_e, layer_input, d_resid),
    )
    all_acts, (cross_all, small_sum, grad_x) = results[:n_act], results[n_act:]
    my_dp = lax.axis_index("dp")
    over_tokens = (((0,), (0,)), ((), ()))
    grads = [[] for _ in range(6)]
    for layer in range(layer_count):
        context_t, act_t, dqkv_t, d_pre_t = all_acts[4 * layer : 4 * layer + 4]
        unit_t = cross_all[:, layer, 0].reshape(total_rows, dp_width).astype(f32)
        d_t = cross_all[:, layer, 1].reshape(total_rows, dp_width)

        def here(vector):
            return lax.dynamic_slice_in_dim(vector[layer], my_dp * dp_width, dp_width)

        a_t = (unit_t * here(gain_one) + here(bias_one)).astype(bf16)
        m_t = (unit_t * here(gain_two) + here(bias_two)).astype(bf16)

        def contract(left, right):
            return lax.dot_general(left, right, over_tokens, preferred_element_type=f32)

        qkv_sums = jnp.sum(dqkv_t.astype(f32), axis=0).reshape(3, -1)
        fc_sums = jnp.sum(d_pre_t.astype(f32), axis=0)
        grads[0].append(contract(a_t, dqkv_t).reshape(w_qkv.shape[1:]))
        grads[1].append(
            lax.dynamic_slice_in_dim(qkv_sums, my_dp * b_qkv.shape[2], b_qkv.shape[2], axis=1)
        )
        grads[2].append(contract(context_t, d_t))
        grads[3].append(contract(m_t, d_pre_t))
        grads[4].append(lax.dynamic_slice_in_dim(fc_sums, my_dp * b_fc.shape[1], b_fc.shape[1]))
        grads[5].append(contract(act_t, d_t))
    stacked_grads = tuple(jnp.stack(group) for group in grads)
    vector_grads = lax.dynamic_slice_in_dim(
        small_sum[:n_sums].reshape(layer_count, 5, dp_width), my_tensor * vec_width, vec_width, axis=2
    )
    return (
        y_out,
        grad_x,
        vector_grads[:, 0],
        vector_grads[:, 1],
        vector_grads[:, 2],
        vector_grads[:, 3],
        vector_grads[:, 4],
    ) + stacked_grads


def solution(mesh):
    in_specs = (
        P(("dp", "tensor"), None),
        P("dp", None),
        P(None, ("dp", "tensor")),
        P(None, ("dp", "tensor")),
        P(None, ("dp", "tensor")),
        P(None, ("dp", "tensor")),
        P(None, ("dp", "tensor")),
        P(None, "dp", None, "tensor"),
        P(None, None, ("tensor", "dp")),
        P(None, "tensor", "dp"),
        P(None, "dp", "tensor"),
        P(None, ("tensor", "dp")),
        P(None, "tensor", "dp"),
        P(("dp", "tensor"), None),
    )
    out_specs = (
        P(("dp", "tensor"), None),
        P(("dp", "tensor"), None),
        P(None, ("dp", "tensor")),
        P(None, ("dp", "tensor")),
        P(None, ("dp", "tensor")),
        P(None, ("dp", "tensor")),
        P(None, ("dp", "tensor")),
        P(None, "dp", None, "tensor"),
        P(None, None, ("tensor", "dp")),
        P(None, "tensor", "dp"),
        P(None, "dp", "tensor"),
        P(None, ("tensor", "dp")),
        P(None, "tensor", "dp"),
    )
    return jax.shard_map(
        per_device, mesh=mesh, in_specs=in_specs, out_specs=out_specs, check_vma=False
    )
```

```python
import functools

import jax
import jax.numpy as jnp
from jax import lax
from jax.experimental import pallas as pl
from jax.experimental.pallas import tpu as pltpu
from jax.sharding import PartitionSpec as P

HD = 64
ROT = 16


EPS = 1e-05
NEG_FILL = -1e30


def gelu_exact(values):
    return 0.5 * values * (1.0 + jax.scipy.special.erf(values * 0.7071067811865476))


def gelu_slope(values):
    normal_cdf = 0.5 * (1.0 + jax.scipy.special.erf(values * 0.7071067811865476))
    return normal_cdf + values * jnp.exp(-0.5 * values * values) * 0.3989422804014327


def group_layout(seq_len, total_rows):
    ends = jnp.cumsum(seq_len)
    starts = ends - seq_len
    row_ids = jnp.arange(total_rows, dtype=jnp.int32)
    member = (row_ids[:, None] >= starts[None, :]) & (row_ids[:, None] < ends[None, :])
    seq_index = jnp.arange(seq_len.shape[0], dtype=jnp.int32)
    seq_ids = jnp.sum(jnp.where(member, seq_index[None, :], 0), axis=1)
    row_start = jnp.sum(jnp.where(member, starts[None, :], 0), axis=1)
    return (seq_ids, row_ids - row_start, row_ids)


def rotary_tables(positions):
    half_rot = ROT // 2
    freq_ids = jnp.arange(half_rot, dtype=jnp.float32)
    inverse = jnp.power(10000.0, -2.0 * freq_ids / ROT)
    angles = positions.astype(jnp.float32)[:, None] * inverse[None, :]
    return (jnp.cos(angles), jnp.sin(angles))


def rotate(vectors, cos_tab, sin_tab, direction_sign):
    half_rot = ROT // 2
    lower_half = vectors[..., :half_rot]
    upper_half = vectors[..., half_rot:ROT]
    cos_b = cos_tab[:, None, :]
    sin_b = sin_tab[:, None, :]
    new_lower = lower_half * cos_b - direction_sign * upper_half * sin_b
    new_upper = upper_half * cos_b + direction_sign * lower_half * sin_b
    return jnp.concatenate([new_lower, new_upper, vectors[..., ROT:]], axis=-1)


def masked_block(q_blk, keys, q_seq, q_row, seq_ids, row_ids):
    scores = jnp.einsum("qhd,khd->hqk", q_blk, keys, preferred_element_type=jnp.float32) * HD ** (
        -0.5
    )
    allowed = (q_seq[:, None] == seq_ids[None, :]) & (row_ids[None, :] <= q_row[:, None])
    return jnp.where(allowed[None], scores, NEG_FILL)


def attention_forward(queries, keys, values, seq_ids, row_ids):
    total_rows, heads_here, head_dim = queries.shape
    block_rows = min(512, total_rows)
    blocks = total_rows // block_rows

    def one_block(inputs):
        q_blk, q_seq, q_row = inputs
        scores = masked_block(q_blk, keys, q_seq, q_row, seq_ids, row_ids)
        top_val = jnp.max(scores, axis=-1, keepdims=True)
        exponent_terms = jnp.exp(scores - top_val)
        totals = jnp.sum(exponent_terms, axis=-1, keepdims=True)
        attn_probs = (exponent_terms / totals).astype(jnp.bfloat16)
        context = jnp.einsum(
            "hqk,khd->qhd", attn_probs, values, preferred_element_type=jnp.float32
        ).astype(jnp.bfloat16)
        return (context, (top_val + jnp.log(totals))[..., 0])

    contexts, log_totals = lax.map(
        one_block,
        (
            queries.reshape(blocks, block_rows, heads_here, head_dim),
            seq_ids.reshape(blocks, block_rows),
            row_ids.reshape(blocks, block_rows),
        ),
    )
    return (contexts.reshape(total_rows, heads_here, head_dim), log_totals)


def attention_backward(queries, keys, values, contexts, d_context, log_totals, seq_ids, row_ids):
    total_rows, heads_here, head_dim = queries.shape
    block_rows = min(512, total_rows)
    blocks = total_rows // block_rows

    def one_block(carry, inputs):
        d_keys, d_values = carry
        q_blk, c_blk, dc_blk, lse_blk, q_seq, q_row = inputs
        scores = masked_block(q_blk, keys, q_seq, q_row, seq_ids, row_ids)
        probs_full = jnp.exp(scores - lse_blk[..., None])
        d_probs = jnp.einsum("qhd,khd->hqk", dc_blk, values, preferred_element_type=jnp.float32)
        delta = jnp.sum(dc_blk.astype(jnp.float32) * c_blk.astype(jnp.float32), axis=-1)
        d_scores = probs_full * (d_probs - jnp.transpose(delta)[:, :, None])
        d_scaled = (d_scores * HD ** (-0.5)).astype(jnp.bfloat16)
        d_q = jnp.einsum("hqk,khd->qhd", d_scaled, keys, preferred_element_type=jnp.float32)
        d_keys = d_keys + jnp.einsum(
            "hqk,qhd->khd", d_scaled, q_blk, preferred_element_type=jnp.float32
        )
        d_values = d_values + jnp.einsum(
            "hqk,qhd->khd",
            probs_full.astype(jnp.bfloat16),
            dc_blk,
            preferred_element_type=jnp.float32,
        )
        return ((d_keys, d_values), d_q)

    zero_keys = jnp.zeros(keys.shape, jnp.float32)
    shape_blk = (blocks, block_rows, heads_here, head_dim)
    carry_out, d_queries = lax.scan(
        one_block,
        (zero_keys, zero_keys),
        (
            queries.reshape(shape_blk),
            contexts.reshape(shape_blk),
            d_context.reshape(shape_blk),
            log_totals,
            seq_ids.reshape(blocks, block_rows),
            row_ids.reshape(blocks, block_rows),
        ),
    )
    return (d_queries.reshape(total_rows, heads_here, head_dim), carry_out[0], carry_out[1])


MESH = pl.DeviceIdType.MESH
ANY = pl.BlockSpec(memory_space=pl.ANY)
VMEM = pl.BlockSpec(memory_space=pltpu.VMEM)
N_SEMS = 160
N_LOCAL = 32


class Links:
    def __init__(self, n_dp, n_tensor, send_sems, recv_sems, local_sems):
        self.n_dp, self.n_tensor = n_dp, n_tensor
        self.dp, self.tensor = lax.axis_index("dp"), lax.axis_index("tensor")
        self.send_sems, self.recv_sems, self.local_sems = send_sems, recv_sems, local_sems
        self.used, self.used_local = 0, 0
        self.sent = []

    def send(self, src, dst, **where):
        copy = pltpu.make_async_remote_copy(
            src_ref=src,
            dst_ref=dst,
            send_sem=self.send_sems.at[self.used],
            recv_sem=self.recv_sems.at[self.used],
            device_id=where,
            device_id_type=MESH,
        )
        self.used += 1
        copy.start()
        self.sent.append(copy)
        return copy

    def local(self, src, dst):
        copy = pltpu.make_async_copy(src, dst, self.local_sems.at[self.used_local])
        self.used_local += 1
        copy.start()
        return copy

    def dp_peer(self, step):
        return lax.rem(self.dp + step, self.n_dp)

    def tensor_peer(self, step):
        return lax.rem(self.tensor + step, self.n_tensor)

    def tensor_from(self, step):
        return lax.rem(self.tensor + self.n_tensor - step, self.n_tensor)

    def barrier(self, with_dp):
        sem = pltpu.get_barrier_semaphore()
        count = self.n_tensor - 1
        for step in range(1, self.n_tensor):
            pl.semaphore_signal(
                sem, inc=1, device_id={"tensor": self.tensor_peer(step)}, device_id_type=MESH
            )
        if with_dp:
            count += self.n_dp - 1
            for step in range(1, self.n_dp):
                pl.semaphore_signal(
                    sem, inc=1, device_id={"dp": self.dp_peer(step)}, device_id_type=MESH
                )
        pl.semaphore_wait(sem, count)

    def finish(self):
        for copy in self.sent:
            copy.wait_send()


class DpGather:
    def __init__(self, links, items):
        self.links = links
        self.chips = links.n_dp // 2
        self.core, self.chip = lax.rem(links.dp, 2), links.dp // 2
        self.partner = links.dp + 1 - 2 * self.core
        self.relay = self.chips == 4
        self.whole = items
        self.pieces = []
        for own, slot in items:
            rows = own.shape[0] // 2
            for half in range(2):
                self.pieces.append((own, slot, pl.ds(half * rows, rows), half))
        if self.relay:
            near = self.chip + 1 - 2 * lax.rem(self.chip, 2)
            far = lax.rem(self.chip + 2, 4)
            self.across = lax.rem(near + 2, 4)
            self.order = ((near, far), (far, near))
            self.first = [self.out(piece, self.order[piece[3]][0]) for piece in self.pieces]
            self.second = [self.out(piece, self.order[piece[3]][1]) for piece in self.pieces]
        else:
            self.direct = [
                [self.out(piece, lax.rem(self.chip + step, self.chips)) for piece in self.pieces]
                for step in range(1, self.chips)
            ]
        self.passed = [
            links.send(own, slot(links.dp), dp=self.partner) for own, slot in items
        ]
        self.kept = [links.local(own, slot(links.dp)) for own, slot in items]

    def device(self, chip):
        return chip * 2 + self.core

    def out(self, piece, chip):
        own, slot, rows, _ = piece
        return self.links.send(
            own.at[rows], slot(self.links.dp).at[rows], dp=self.device(chip)
        )

    def pass_on(self, piece, chip, target):
        _, slot, rows, _ = piece
        block = slot(self.device(chip)).at[rows]
        return self.links.send(block, block, dp=target)

    def finish(self):
        if self.relay:
            relayed = []
            for copy, piece in zip(self.first, self.pieces):
                origin, target = self.order[piece[3]]
                copy.wait_recv()
                relayed.append(self.pass_on(piece, origin, self.device(target)))
                self.passed.append(self.pass_on(piece, origin, self.partner))
            for copy, piece in zip(self.second, self.pieces):
                copy.wait_recv()
                self.passed.append(self.pass_on(piece, self.order[piece[3]][1], self.partner))
            for copy, piece in zip(relayed, self.pieces):
                copy.wait_recv()
                self.passed.append(self.pass_on(piece, self.across, self.partner))
        else:
            for step, copies in enumerate(self.direct):
                origin = lax.rem(self.chip + self.chips - step - 1, self.chips)
                for copy, piece in zip(copies, self.pieces):
                    copy.wait_recv()
                    self.passed.append(self.pass_on(piece, origin, self.partner))
        for copy in self.passed:
            copy.wait_recv()
        for copy in self.kept:
            copy.wait()


def row_slot(ref, rows):
    return lambda d: ref.at[pl.ds(pl.multiple_of(d * rows, rows), rows)]


def weight_slot(ref, axis, size):
    if axis is None:
        return lambda d: ref.at[d]
    if axis == 0:
        return lambda d: ref.at[pl.ds(pl.multiple_of(d * size, size), size), :]
    return lambda d: ref.at[:, pl.ds(pl.multiple_of(d * size, size), size)]


def weight_items(held, outs, axes):
    return [
        (own, weight_slot(ref, axis, own.shape[axis] if axis is not None else 0))
        for own, ref, axis in zip(held, outs, axes)
    ]


def scratch_sems():
    return [
        pltpu.SemaphoreType.DMA((N_SEMS,)),
        pltpu.SemaphoreType.DMA((N_SEMS,)),
        pltpu.SemaphoreType.DMA((N_LOCAL,)),
    ]


def entry_kernel(n_dp, n_tensor, axes, *refs):
    n_w = len(axes)
    w_in, (small_in, x_in, d_in) = refs[:n_w], refs[n_w : n_w + 3]
    w_out, refs = refs[n_w + 3 : 2 * n_w + 3], refs[2 * n_w + 3 :]
    (small_out, unit_out, rows_out), refs = refs[:3], refs[3:]
    held, refs = refs[:n_w], refs[n_w:]
    unit_own, rows_own = refs[:2]
    links = Links(n_dp, n_tensor, *refs[2:])
    loads = [links.local(src.at[0], dst) for src, dst in zip(w_in, held)]
    links.barrier(True)
    for copy in loads:
        copy.wait()
    weights = DpGather(links, weight_items(held, w_out, axes))
    small_own = links.local(small_in, small_out.at[links.tensor, links.dp])
    small_sent = [
        links.send(small_in, small_out.at[links.tensor, links.dp], dp=links.dp_peer(step))
        for step in range(1, n_dp)
    ]
    unit_own[...] = unit_rows(x_in[...])[0].astype(jnp.bfloat16)
    rows_own[...] = d_in[...].astype(jnp.bfloat16)
    unit_sent, unit_kept = start_gather(links, unit_out, unit_own)
    rows_sent, rows_kept = start_gather(links, rows_out, rows_own)
    small_own.wait()
    for copy in small_sent:
        copy.wait_recv()
    small_wide = [
        links.send(
            small_out.at[links.tensor], small_out.at[links.tensor], tensor=links.tensor_peer(step)
        )
        for step in range(1, n_tensor)
    ]
    weights.finish()
    for copy in unit_sent + rows_sent + small_wide:
        copy.wait_recv()
    unit_kept.wait()
    rows_kept.wait()
    links.finish()


def start_scatter(links, part, landing):
    rows = landing.shape[1]
    return [
        links.send(
            row_slot(part, rows)(links.tensor_peer(step)),
            landing.at[step - 1],
            tensor=links.tensor_peer(step),
        )
        for step in range(1, links.n_tensor)
    ]


def end_scatter(links, part, landing, copies):
    rows = landing.shape[1]
    total = part[pl.ds(pl.multiple_of(links.tensor * rows, rows), rows), :].astype(jnp.float32)
    for step, copy in enumerate(copies):
        copy.wait_recv()
        total = total + landing[step].astype(jnp.float32)
    return total


def start_gather(links, out, own):
    rows = own.shape[0]
    slot = row_slot(out, rows)
    copies = [
        links.send(own, slot(links.tensor), tensor=links.tensor_peer(step))
        for step in range(1, links.n_tensor)
    ]
    return copies, links.local(own, slot(links.tensor))


def unit_rows(values):
    average = jnp.mean(values, axis=-1, keepdims=True)
    centred = values - average
    variance = jnp.mean(centred * centred, axis=-1, keepdims=True)
    scale = lax.rsqrt(variance + EPS)
    return centred * scale, scale


def back_unit(values, grad):
    unit, scale = unit_rows(values)
    return scale * (
        grad
        - jnp.mean(grad, axis=-1, keepdims=True)
        - unit * jnp.mean(grad * unit, axis=-1, keepdims=True)
    )


def forward_kernel(n_dp, n_tensor, axes, layer, part, resid, bias, *refs):
    n_w = len(axes)
    w_in, refs = refs[:n_w], refs[n_w:]
    new_resid, rows_out = refs[:2]
    w_out, refs = refs[2 : 2 + n_w], refs[2 + n_w :]
    landing, own = refs[:2]
    held, refs = refs[2 : 2 + n_w], refs[2 + n_w :]
    links = Links(n_dp, n_tensor, *refs)
    loads = [links.local(src.at[layer + 1], dst) for src, dst in zip(w_in, held)]
    links.barrier(True)
    copies = start_scatter(links, part, landing)
    for copy in loads:
        copy.wait()
    weights = DpGather(links, weight_items(held, w_out, axes))
    branch = end_scatter(links, part, landing, copies)
    values = resid[...] + branch + bias[...]
    new_resid[...] = values
    own[...] = unit_rows(values)[0].astype(jnp.bfloat16)
    copies, local = start_gather(links, rows_out, own)
    weights.finish()
    for copy in copies:
        copy.wait_recv()
    local.wait()
    links.finish()


def backward_kernel(n_dp, n_tensor, n_act, last, *refs):
    acts, refs = refs[:n_act], refs[n_act:]
    part_e, resid, dres = refs[:3]
    refs = refs[3:]
    if last:
        (part_y, bias), refs = refs[:2], refs[2:]
    act_out, refs = refs[:n_act], refs[n_act:]
    (d_out, rows_out), refs = refs[:2], refs[2:]
    if last:
        y_out, refs = refs[0], refs[1:]
    held, refs = refs[:n_act], refs[n_act:]
    (land_e, own), refs = refs[:2], refs[2:]
    if last:
        land_y, refs = refs[0], refs[1:]
    links = Links(n_dp, n_tensor, *refs)
    loads = [links.local(src, dst) for src, dst in zip(acts, held)]
    links.barrier(True)
    copies_e = start_scatter(links, part_e, land_e)
    if last:
        copies_y = start_scatter(links, part_y, land_y)
    for copy in loads:
        copy.wait()
    gathered = DpGather(
        links, [(block, row_slot(ref, block.shape[0])) for block, ref in zip(held, act_out)]
    )
    grad = end_scatter(links, part_e, land_e, copies_e)
    values = resid[...]
    new_d = dres[...] + back_unit(values, grad)
    d_out[...] = new_d
    own[...] = new_d.astype(jnp.bfloat16)
    copies, local = start_gather(links, rows_out, own)
    if last:
        y_out[...] = values + end_scatter(links, part_y, land_y, copies_y) + bias[...]
    gathered.finish()
    for copy in copies:
        copy.wait_recv()
    local.wait()
    links.finish()


def exit_kernel(n_dp, n_tensor, n_act, *refs):
    acts, refs = refs[:n_act], refs[n_act:]
    cross, small, part_e, resid, dres = refs[:5]
    act_out, refs = refs[5 : 5 + n_act], refs[5 + n_act :]
    cross_out, small_out, d_out = refs[:3]
    held, refs = refs[3 : 3 + n_act], refs[3 + n_act :]
    land_e, land_s, half_s, land_t = refs[:4]
    links = Links(n_dp, n_tensor, *refs[4:])
    loads = [links.local(src, dst) for src, dst in zip(acts, held)]
    links.barrier(True)
    copies_e = start_scatter(links, part_e, land_e)
    small_sent = [
        links.send(small.at[links.dp_peer(step)], land_s.at[step - 1], dp=links.dp_peer(step))
        for step in range(1, n_dp)
    ]
    for copy in loads:
        copy.wait()
    items = [
        (own, row_slot(ref, own.shape[0])) for own, ref in zip(held, act_out)
    ]
    gathered = DpGather(links, items)
    cross_sent = [
        links.send(cross.at[links.dp_peer(step)], cross_out.at[links.dp], dp=links.dp_peer(step))
        for step in range(1, n_dp)
    ]
    cross_kept = links.local(cross.at[links.dp], cross_out.at[links.dp])
    total = small[links.dp]
    for step, copy in enumerate(small_sent):
        copy.wait_recv()
        total = total + land_s[step]
    half_s[...] = total
    wide = [
        links.send(half_s, land_t.at[step - 1], tensor=links.tensor_peer(step))
        for step in range(1, n_tensor)
    ]
    grad = end_scatter(links, part_e, land_e, copies_e)
    d_out[...] = dres[...] + back_unit(resid[...], grad)
    for step, copy in enumerate(wide):
        copy.wait_recv()
        total = total + land_t[step]
    small_out[...] = total
    gathered.finish()
    for copy in cross_sent:
        copy.wait_recv()
    cross_kept.wait()
    links.finish()


def call(kernel, name, collective, outs, out_specs, in_specs, scratch, args):
    return pl.pallas_call(
        kernel,
        out_shape=outs,
        in_specs=in_specs,
        out_specs=out_specs,
        scratch_shapes=scratch + scratch_sems(),
        name=name,
        compiler_params=pltpu.CompilerParams(
            collective_id=collective, has_side_effects=True, vmem_limit_bytes=40 << 20
        ),
    )(*args)


def shaped(shape, dtype):
    return jax.ShapeDtypeStruct(tuple(shape), dtype)


def pack_rows(parts):
    flat = jnp.concatenate([part.reshape(-1) for part in parts])
    padded = -(-flat.shape[0] // 1024) * 1024
    return jnp.pad(flat, (0, padded - flat.shape[0])).reshape(-1, 128)


def per_device(
    x_in,
    seq_lengths,
    ln1_gain,
    ln1_bias,
    ln2_gain,
    ln2_bias,
    res_bias,
    w_qkv,
    b_qkv,
    w_out,
    w_fc,
    b_fc,
    w_proj,
    grad_out,
):
    n_tensor, n_dp = lax.axis_size("tensor"), lax.axis_size("dp")
    my_tensor = lax.axis_index("tensor")
    bf16, f32 = jnp.bfloat16, jnp.float32
    my_rows, width = x_in.shape
    group_rows = my_rows * n_tensor
    total_rows = group_rows * n_dp
    layer_count = w_qkv.shape[0]
    heads_here = w_qkv.shape[3] // HD
    dp_width = width // n_dp
    vec_width = dp_width // n_tensor

    columns_ok = dp_width % 128 == 0
    shards = (w_qkv.reshape(layer_count, dp_width, -1), w_out, w_fc, w_proj)
    axes = (0, 1 if columns_ok else None, 0, 1 if columns_ok else None)
    gathered = []
    for shard, axis in zip(shards, axes):
        shape = list(shard.shape[1:])
        if axis is None:
            shape = [n_dp] + shape
        else:
            shape[axis] *= n_dp
        gathered.append(shaped(shape, bf16))
    smalls = (
        jnp.stack([ln1_gain, ln1_bias, ln2_gain, ln2_bias, res_bias]),
        b_qkv,
        b_fc,
    )
    packed = pack_rows(smalls)
    unit_shape, d_shape = shaped((group_rows, width), bf16), shaped(x_in.shape, f32)
    own_rows = pltpu.VMEM((my_rows, width), bf16)
    land = pltpu.VMEM((n_tensor - 1, my_rows, width), bf16)
    held = [pltpu.VMEM(shard.shape[1:], bf16) for shard in shards]
    entry = call(
        functools.partial(entry_kernel, n_dp, n_tensor, axes),
        "entry",
        0,
        tuple(gathered)
        + (shaped((n_tensor, n_dp) + packed.shape, f32), unit_shape, unit_shape),
        (ANY,) * 4 + (VMEM,) * 3,
        [ANY] * 4 + [VMEM] * 3,
        held + [own_rows] * 2,
        shards + (packed, x_in, grad_out),
    )
    small_all, unit_full, d_rows = entry[4:]

    def in_columns(matrix):
        if matrix.ndim == 2:
            return matrix
        return jnp.transpose(matrix, (1, 0, 2)).reshape(-1, width)

    weights = [tuple(in_columns(matrix) for matrix in entry[:4])]
    small_all = small_all.reshape(n_tensor, n_dp, -1)
    n_gain = smalls[0].size
    vectors = jnp.transpose(
        small_all[:, :, :n_gain].reshape(n_tensor, n_dp, 5, layer_count, vec_width),
        (2, 3, 1, 0, 4),
    ).reshape(5, layer_count, width)
    gain_one, bias_one, gain_two, bias_two, out_bias = vectors
    mine = lax.dynamic_index_in_dim(small_all, my_tensor, 0, keepdims=False)
    qkv_vecs = jnp.transpose(
        mine[:, n_gain : n_gain + b_qkv.size].reshape((n_dp,) + b_qkv.shape), (1, 2, 0, 3)
    ).reshape(layer_count, 1, -1)
    fc_vecs = jnp.transpose(
        mine[:, n_gain + b_qkv.size : n_gain + b_qkv.size + b_fc.size].reshape(
            (n_dp,) + b_fc.shape
        ),
        (1, 0, 2),
    ).reshape(layer_count, 1, -1)

    seq_ids, positions, row_ids = group_layout(seq_lengths[0], group_rows)
    cos_tab, sin_tab = rotary_tables(positions)
    resid = x_in
    saved = []
    for layer in range(layer_count):
        qkv_mat, out_mat, fc_mat, proj_mat = weights[layer]
        unit_wide = unit_full.astype(f32)
        normed_a = (unit_wide * gain_one[layer] + bias_one[layer]).astype(bf16)
        normed_m = (unit_wide * gain_two[layer] + bias_two[layer]).astype(bf16)
        projected = (
            jnp.dot(normed_a, qkv_mat, preferred_element_type=f32) + qkv_vecs[layer]
        )
        split_heads = projected.reshape(group_rows, 3, heads_here, HD)
        queries = rotate(split_heads[:, 0], cos_tab, sin_tab, 1.0).astype(bf16)
        keys = rotate(split_heads[:, 1], cos_tab, sin_tab, 1.0).astype(bf16)
        values = split_heads[:, 2].astype(bf16)
        contexts, log_totals = attention_forward(queries, keys, values, seq_ids, row_ids)
        hidden_pre = jnp.dot(normed_m, fc_mat, preferred_element_type=f32) + fc_vecs[layer]
        activated = gelu_exact(hidden_pre).astype(bf16)
        flat_context = contexts.reshape(group_rows, -1)
        partial = (
            jnp.dot(flat_context, out_mat, preferred_element_type=f32)
            + jnp.dot(activated, proj_mat, preferred_element_type=f32)
        ).astype(bf16)
        saved.append(
            (resid, unit_full, queries, keys, values, contexts, log_totals, hidden_pre, activated)
        )
        if layer + 1 < layer_count:
            stepped = call(
                functools.partial(forward_kernel, n_dp, n_tensor, axes, layer),
                f"forward{layer}",
                1 + layer,
                (d_shape, unit_shape) + tuple(gathered),
                (VMEM,) * 2 + (ANY,) * 4,
                [VMEM] * 3 + [ANY] * 4,
                [land, own_rows] + held,
                (partial, resid, out_bias[layer][None]) + shards,
            )
            resid, unit_full = stepped[:2]
            weights.append(tuple(in_columns(matrix) for matrix in stepped[2:]))
    d_resid = grad_out
    acts, cross, sums = [None] * layer_count, [None] * layer_count, [None] * layer_count
    all_acts = [None] * layer_count
    for layer in reversed(range(layer_count)):
        (
            layer_input,
            unit_full,
            queries,
            keys,
            values,
            contexts,
            log_totals,
            hidden_pre,
            activated,
        ) = saved[layer]
        qkv_mat, out_mat, fc_mat, proj_mat = weights[layer]
        out_bias_grad = jnp.sum(d_resid, axis=0)
        flat_context = contexts.reshape(group_rows, -1)
        transposed = (((1,), (1,)), ((), ()))
        d_context = lax.dot_general(
            d_rows, out_mat, transposed, preferred_element_type=f32
        ).astype(bf16)
        d_act = lax.dot_general(d_rows, proj_mat, transposed, preferred_element_type=f32)
        d_pre_b = (d_act * gelu_slope(hidden_pre)).astype(bf16)
        d_queries, d_keys, d_values = attention_backward(
            queries,
            keys,
            values,
            contexts,
            d_context.reshape(group_rows, heads_here, HD),
            log_totals,
            seq_ids,
            row_ids,
        )
        d_queries = rotate(d_queries, cos_tab, sin_tab, -1.0)
        d_keys = rotate(d_keys, cos_tab, sin_tab, -1.0)
        flat_dqkv = (
            jnp.stack([d_queries, d_keys, d_values], axis=1).reshape(group_rows, -1).astype(bf16)
        )
        d_a = lax.dot_general(flat_dqkv, qkv_mat, transposed, preferred_element_type=f32)
        d_m = lax.dot_general(d_pre_b, fc_mat, transposed, preferred_element_type=f32)
        unit_wide = unit_full.astype(f32)
        sums[layer] = (
            jnp.sum(d_a * unit_wide, axis=0),
            jnp.sum(d_a, axis=0),
            jnp.sum(d_m * unit_wide, axis=0),
            jnp.sum(d_m, axis=0),
            out_bias_grad,
        )
        part_e = (d_a * gain_one[layer] + d_m * gain_two[layer]).astype(bf16)
        acts[layer] = (flat_context, activated, flat_dqkv, d_pre_b)
        cross[layer] = jnp.stack([unit_full, d_rows]).reshape(2, group_rows, n_dp, dp_width)
        if layer > 0:
            last = layer + 1 == layer_count
            n_act = len(acts[layer])
            stepped = call(
                functools.partial(backward_kernel, n_dp, n_tensor, n_act, last),
                f"backward{layer}",
                layer_count + layer,
                tuple(shaped((total_rows, array.shape[1]), bf16) for array in acts[layer])
                + (d_shape, unit_shape)
                + ((d_shape,) if last else ()),
                (ANY,) * n_act + (VMEM,) * (3 if last else 2),
                [ANY] * n_act + [VMEM] * (5 if last else 3),
                [pltpu.VMEM(array.shape, bf16) for array in acts[layer]]
                + [land, own_rows]
                + ([land] if last else []),
                acts[layer]
                + (part_e, layer_input, d_resid)
                + ((partial, out_bias[layer][None]) if last else ()),
            )
            all_acts[layer] = stepped[:n_act]
            d_resid, d_rows = stepped[n_act : n_act + 2]
            if last:
                y_out = stepped[n_act + 2]
    flat_acts = acts[0]
    n_act = len(flat_acts)
    cross_in = jnp.transpose(jnp.stack(cross), (3, 0, 1, 2, 4))
    stacked = jnp.stack([jnp.stack(group) for group in sums]).reshape(-1, width)
    n_sums = stacked.shape[0]
    padded = -(-n_sums // 8) * 8
    small_in = jnp.transpose(
        jnp.pad(stacked, ((0, padded - n_sums), (0, 0))).reshape(padded, n_dp, dp_width), (1, 0, 2)
    )
    small_block = (padded, dp_width)
    results = call(
        functools.partial(exit_kernel, n_dp, n_tensor, n_act),
        "exit",
        2 * layer_count,
        tuple(shaped((total_rows, array.shape[1]), bf16) for array in flat_acts)
        + (shaped(cross_in.shape, bf16), shaped(small_block, f32), shaped(x_in.shape, f32)),
        (ANY,) * n_act + (VMEM,) * 3,
        [ANY] * n_act + [VMEM] * 5,
        [pltpu.VMEM(array.shape, bf16) for array in flat_acts]
        + [
            land,
            pltpu.VMEM((n_dp - 1,) + small_block, f32),
            pltpu.VMEM(small_block, f32),
            pltpu.VMEM((n_tensor - 1,) + small_block, f32),
        ],
        tuple(flat_acts) + (cross_in, small_in, part_e, layer_input, d_resid),
    )
    all_acts[0], (cross_all, small_sum, grad_x) = results[:n_act], results[n_act:]
    my_dp = lax.axis_index("dp")
    over_tokens = (((0,), (0,)), ((), ()))
    grads = [[] for _ in range(6)]
    for layer in range(layer_count):
        context_t, act_t, dqkv_t, d_pre_t = all_acts[layer]
        unit_t = cross_all[:, layer, 0].reshape(total_rows, dp_width).astype(f32)
        d_t = cross_all[:, layer, 1].reshape(total_rows, dp_width)

        def here(vector):
            return lax.dynamic_slice_in_dim(vector[layer], my_dp * dp_width, dp_width)

        a_t = (unit_t * here(gain_one) + here(bias_one)).astype(bf16)
        m_t = (unit_t * here(gain_two) + here(bias_two)).astype(bf16)

        def contract(left, right):
            return lax.dot_general(left, right, over_tokens, preferred_element_type=f32)

        qkv_sums = jnp.sum(dqkv_t.astype(f32), axis=0).reshape(3, -1)
        fc_sums = jnp.sum(d_pre_t.astype(f32), axis=0)
        grads[0].append(contract(a_t, dqkv_t).reshape(w_qkv.shape[1:]))
        grads[1].append(
            lax.dynamic_slice_in_dim(qkv_sums, my_dp * b_qkv.shape[2], b_qkv.shape[2], axis=1)
        )
        grads[2].append(contract(context_t, d_t))
        grads[3].append(contract(m_t, d_pre_t))
        grads[4].append(lax.dynamic_slice_in_dim(fc_sums, my_dp * b_fc.shape[1], b_fc.shape[1]))
        grads[5].append(contract(act_t, d_t))
    stacked_grads = tuple(jnp.stack(group) for group in grads)
    vector_grads = lax.dynamic_slice_in_dim(
        small_sum[:n_sums].reshape(layer_count, 5, dp_width), my_tensor * vec_width, vec_width, axis=2
    )
    return (
        y_out,
        grad_x,
        vector_grads[:, 0],
        vector_grads[:, 1],
        vector_grads[:, 2],
        vector_grads[:, 3],
        vector_grads[:, 4],
    ) + stacked_grads


def solution(mesh):
    in_specs = (
        P(("dp", "tensor"), None),
        P("dp", None),
        P(None, ("dp", "tensor")),
        P(None, ("dp", "tensor")),
        P(None, ("dp", "tensor")),
        P(None, ("dp", "tensor")),
        P(None, ("dp", "tensor")),
        P(None, "dp", None, "tensor"),
        P(None, None, ("tensor", "dp")),
        P(None, "tensor", "dp"),
        P(None, "dp", "tensor"),
        P(None, ("tensor", "dp")),
        P(None, "tensor", "dp"),
        P(("dp", "tensor"), None),
    )
    out_specs = (
        P(("dp", "tensor"), None),
        P(("dp", "tensor"), None),
        P(None, ("dp", "tensor")),
        P(None, ("dp", "tensor")),
        P(None, ("dp", "tensor")),
        P(None, ("dp", "tensor")),
        P(None, ("dp", "tensor")),
        P(None, "dp", None, "tensor"),
        P(None, None, ("tensor", "dp")),
        P(None, "tensor", "dp"),
        P(None, "dp", "tensor"),
        P(None, ("tensor", "dp")),
        P(None, "tensor", "dp"),
    )
    return jax.shard_map(
        per_device, mesh=mesh, in_specs=in_specs, out_specs=out_specs, check_vma=False
    )
```

```python
import functools

import jax
import jax.numpy as jnp
from jax import lax
from jax.experimental import pallas as pl
from jax.experimental.pallas import tpu as pltpu
from jax.sharding import PartitionSpec as P

HD = 64
ROT = 16


EPS = 1e-05
NEG_FILL = -1e30


def gelu_exact(values):
    return 0.5 * values * (1.0 + jax.scipy.special.erf(values * 0.7071067811865476))


def gelu_slope(values):
    normal_cdf = 0.5 * (1.0 + jax.scipy.special.erf(values * 0.7071067811865476))
    return normal_cdf + values * jnp.exp(-0.5 * values * values) * 0.3989422804014327


def group_layout(seq_len, total_rows):
    ends = jnp.cumsum(seq_len)
    starts = ends - seq_len
    row_ids = jnp.arange(total_rows, dtype=jnp.int32)
    member = (row_ids[:, None] >= starts[None, :]) & (row_ids[:, None] < ends[None, :])
    seq_index = jnp.arange(seq_len.shape[0], dtype=jnp.int32)
    seq_ids = jnp.sum(jnp.where(member, seq_index[None, :], 0), axis=1)
    row_start = jnp.sum(jnp.where(member, starts[None, :], 0), axis=1)
    return (seq_ids, row_ids - row_start, row_ids)


def rotary_tables(positions):
    half_rot = ROT // 2
    freq_ids = jnp.arange(half_rot, dtype=jnp.float32)
    inverse = jnp.power(10000.0, -2.0 * freq_ids / ROT)
    angles = positions.astype(jnp.float32)[:, None] * inverse[None, :]
    return (jnp.cos(angles), jnp.sin(angles))


MESH = pl.DeviceIdType.MESH
ANY = pl.BlockSpec(memory_space=pl.ANY)
VMEM = pl.BlockSpec(memory_space=pltpu.VMEM)
N_SEMS = 160
N_LOCAL = 32


class Links:
    def __init__(self, n_dp, n_tensor, send_sems, recv_sems, local_sems):
        self.n_dp, self.n_tensor = n_dp, n_tensor
        self.dp, self.tensor = lax.axis_index("dp"), lax.axis_index("tensor")
        self.send_sems, self.recv_sems, self.local_sems = send_sems, recv_sems, local_sems
        self.used, self.used_local = 0, 0
        self.sent = []

    def send(self, src, dst, **where):
        copy = pltpu.make_async_remote_copy(
            src_ref=src,
            dst_ref=dst,
            send_sem=self.send_sems.at[self.used],
            recv_sem=self.recv_sems.at[self.used],
            device_id=where,
            device_id_type=MESH,
        )
        self.used += 1
        copy.start()
        self.sent.append(copy)
        return copy

    def local(self, src, dst):
        copy = pltpu.make_async_copy(src, dst, self.local_sems.at[self.used_local])
        self.used_local += 1
        copy.start()
        return copy

    def dp_peer(self, step):
        return lax.rem(self.dp + step, self.n_dp)

    def tensor_peer(self, step):
        return lax.rem(self.tensor + step, self.n_tensor)

    def tensor_from(self, step):
        return lax.rem(self.tensor + self.n_tensor - step, self.n_tensor)

    def barrier(self, with_dp):
        sem = pltpu.get_barrier_semaphore()
        count = self.n_tensor - 1
        for step in range(1, self.n_tensor):
            pl.semaphore_signal(
                sem, inc=1, device_id={"tensor": self.tensor_peer(step)}, device_id_type=MESH
            )
        if with_dp:
            count += self.n_dp - 1
            for step in range(1, self.n_dp):
                pl.semaphore_signal(
                    sem, inc=1, device_id={"dp": self.dp_peer(step)}, device_id_type=MESH
                )
        pl.semaphore_wait(sem, count)

    def finish(self):
        for copy in self.sent:
            copy.wait_send()


class DpGather:
    def __init__(self, links, items):
        self.links = links
        self.chips = links.n_dp // 2
        self.core, self.chip = lax.rem(links.dp, 2), links.dp // 2
        self.partner = links.dp + 1 - 2 * self.core
        self.relay = self.chips == 4
        self.whole = items
        self.pieces = []
        for own, slot in items:
            rows = own.shape[0] // 2
            for half in range(2):
                self.pieces.append((own, slot, pl.ds(half * rows, rows), half))
        if self.relay:
            near = self.chip + 1 - 2 * lax.rem(self.chip, 2)
            far = lax.rem(self.chip + 2, 4)
            self.across = lax.rem(near + 2, 4)
            self.order = ((near, far), (far, near))
            self.first = [self.out(piece, self.order[piece[3]][0]) for piece in self.pieces]
            self.second = [self.out(piece, self.order[piece[3]][1]) for piece in self.pieces]
        else:
            self.direct = [
                [self.out(piece, lax.rem(self.chip + step, self.chips)) for piece in self.pieces]
                for step in range(1, self.chips)
            ]
        self.passed = [
            links.send(own, slot(links.dp), dp=self.partner) for own, slot in items
        ]
        self.kept = [links.local(own, slot(links.dp)) for own, slot in items]

    def device(self, chip):
        return chip * 2 + self.core

    def out(self, piece, chip):
        own, slot, rows, _ = piece
        return self.links.send(
            own.at[rows], slot(self.links.dp).at[rows], dp=self.device(chip)
        )

    def pass_on(self, piece, chip, target):
        _, slot, rows, _ = piece
        block = slot(self.device(chip)).at[rows]
        return self.links.send(block, block, dp=target)

    def finish(self):
        if self.relay:
            relayed = []
            for copy, piece in zip(self.first, self.pieces):
                origin, target = self.order[piece[3]]
                copy.wait_recv()
                relayed.append(self.pass_on(piece, origin, self.device(target)))
                self.passed.append(self.pass_on(piece, origin, self.partner))
            for copy, piece in zip(self.second, self.pieces):
                copy.wait_recv()
                self.passed.append(self.pass_on(piece, self.order[piece[3]][1], self.partner))
            for copy, piece in zip(relayed, self.pieces):
                copy.wait_recv()
                self.passed.append(self.pass_on(piece, self.across, self.partner))
        else:
            for step, copies in enumerate(self.direct):
                origin = lax.rem(self.chip + self.chips - step - 1, self.chips)
                for copy, piece in zip(copies, self.pieces):
                    copy.wait_recv()
                    self.passed.append(self.pass_on(piece, origin, self.partner))
        for copy in self.passed:
            copy.wait_recv()
        for copy in self.kept:
            copy.wait()


def row_slot(ref, rows):
    return lambda d: ref.at[pl.ds(pl.multiple_of(d * rows, rows), rows)]


def weight_slot(ref, axis, size):
    if axis is None:
        return lambda d: ref.at[d]
    if axis == 0:
        return lambda d: ref.at[pl.ds(pl.multiple_of(d * size, size), size), :]
    return lambda d: ref.at[:, pl.ds(pl.multiple_of(d * size, size), size)]


def weight_items(held, outs, axes):
    return [
        (own, weight_slot(ref, axis, own.shape[axis] if axis is not None else 0))
        for own, ref, axis in zip(held, outs, axes)
    ]


def scratch_sems():
    return [
        pltpu.SemaphoreType.DMA((N_SEMS,)),
        pltpu.SemaphoreType.DMA((N_SEMS,)),
        pltpu.SemaphoreType.DMA((N_LOCAL,)),
    ]


def entry_kernel(n_dp, n_tensor, axes, *refs):
    n_w = len(axes)
    w_in, (small_in, x_in, d_in) = refs[:n_w], refs[n_w : n_w + 3]
    w_out, refs = refs[n_w + 3 : 2 * n_w + 3], refs[2 * n_w + 3 :]
    (small_out, unit_out, rows_out), refs = refs[:3], refs[3:]
    held, refs = refs[:n_w], refs[n_w:]
    unit_own, rows_own = refs[:2]
    links = Links(n_dp, n_tensor, *refs[2:])
    loads = [links.local(src.at[0], dst) for src, dst in zip(w_in, held)]
    links.barrier(True)
    for copy in loads:
        copy.wait()
    weights = DpGather(links, weight_items(held, w_out, axes))
    small_own = links.local(small_in, small_out.at[links.tensor, links.dp])
    small_sent = [
        links.send(small_in, small_out.at[links.tensor, links.dp], dp=links.dp_peer(step))
        for step in range(1, n_dp)
    ]
    unit_own[...] = unit_rows(x_in[...])[0].astype(jnp.bfloat16)
    rows_own[...] = d_in[...].astype(jnp.bfloat16)
    unit_sent, unit_kept = start_gather(links, unit_out, unit_own)
    rows_sent, rows_kept = start_gather(links, rows_out, rows_own)
    small_own.wait()
    for copy in small_sent:
        copy.wait_recv()
    small_wide = [
        links.send(
            small_out.at[links.tensor], small_out.at[links.tensor], tensor=links.tensor_peer(step)
        )
        for step in range(1, n_tensor)
    ]
    weights.finish()
    for copy in unit_sent + rows_sent + small_wide:
        copy.wait_recv()
    unit_kept.wait()
    rows_kept.wait()
    links.finish()


def start_scatter(links, part, landing):
    rows = landing.shape[1]
    return [
        links.send(
            row_slot(part, rows)(links.tensor_peer(step)),
            landing.at[step - 1],
            tensor=links.tensor_peer(step),
        )
        for step in range(1, links.n_tensor)
    ]


def end_scatter(links, part, landing, copies):
    rows = landing.shape[1]
    total = part[pl.ds(pl.multiple_of(links.tensor * rows, rows), rows), :].astype(jnp.float32)
    for step, copy in enumerate(copies):
        copy.wait_recv()
        total = total + landing[step].astype(jnp.float32)
    return total


def start_gather(links, out, own):
    rows = own.shape[0]
    slot = row_slot(out, rows)
    copies = [
        links.send(own, slot(links.tensor), tensor=links.tensor_peer(step))
        for step in range(1, links.n_tensor)
    ]
    return copies, links.local(own, slot(links.tensor))


def unit_rows(values):
    average = jnp.mean(values, axis=-1, keepdims=True)
    centred = values - average
    variance = jnp.mean(centred * centred, axis=-1, keepdims=True)
    scale = lax.rsqrt(variance + EPS)
    return centred * scale, scale


def back_unit(values, grad):
    unit, scale = unit_rows(values)
    return scale * (
        grad
        - jnp.mean(grad, axis=-1, keepdims=True)
        - unit * jnp.mean(grad * unit, axis=-1, keepdims=True)
    )


def forward_kernel(n_dp, n_tensor, axes, layer, part, resid, bias, *refs):
    n_w = len(axes)
    w_in, refs = refs[:n_w], refs[n_w:]
    new_resid, rows_out = refs[:2]
    w_out, refs = refs[2 : 2 + n_w], refs[2 + n_w :]
    landing, own = refs[:2]
    held, refs = refs[2 : 2 + n_w], refs[2 + n_w :]
    links = Links(n_dp, n_tensor, *refs)
    loads = [links.local(src.at[layer + 1], dst) for src, dst in zip(w_in, held)]
    links.barrier(True)
    copies = start_scatter(links, part, landing)
    for copy in loads:
        copy.wait()
    weights = DpGather(links, weight_items(held, w_out, axes))
    branch = end_scatter(links, part, landing, copies)
    values = resid[...] + branch + bias[...]
    new_resid[...] = values
    own[...] = unit_rows(values)[0].astype(jnp.bfloat16)
    copies, local = start_gather(links, rows_out, own)
    weights.finish()
    for copy in copies:
        copy.wait_recv()
    local.wait()
    links.finish()


def backward_kernel(n_dp, n_tensor, n_act, last, *refs):
    acts, refs = refs[:n_act], refs[n_act:]
    part_e, resid, dres = refs[:3]
    refs = refs[3:]
    if last:
        (part_y, bias), refs = refs[:2], refs[2:]
    act_out, refs = refs[:n_act], refs[n_act:]
    (d_out, rows_out), refs = refs[:2], refs[2:]
    if last:
        y_out, refs = refs[0], refs[1:]
    held, refs = refs[:n_act], refs[n_act:]
    (land_e, own), refs = refs[:2], refs[2:]
    if last:
        land_y, refs = refs[0], refs[1:]
    links = Links(n_dp, n_tensor, *refs)
    loads = [links.local(src, dst) for src, dst in zip(acts, held)]
    links.barrier(True)
    copies_e = start_scatter(links, part_e, land_e)
    if last:
        copies_y = start_scatter(links, part_y, land_y)
    for copy in loads:
        copy.wait()
    gathered = DpGather(
        links, [(block, row_slot(ref, block.shape[0])) for block, ref in zip(held, act_out)]
    )
    grad = end_scatter(links, part_e, land_e, copies_e)
    values = resid[...]
    new_d = dres[...] + back_unit(values, grad)
    d_out[...] = new_d
    own[...] = new_d.astype(jnp.bfloat16)
    copies, local = start_gather(links, rows_out, own)
    if last:
        y_out[...] = values + end_scatter(links, part_y, land_y, copies_y) + bias[...]
    gathered.finish()
    for copy in copies:
        copy.wait_recv()
    local.wait()
    links.finish()


def exit_kernel(n_dp, n_tensor, n_act, *refs):
    acts, refs = refs[:n_act], refs[n_act:]
    cross, small, part_e, resid, dres = refs[:5]
    act_out, refs = refs[5 : 5 + n_act], refs[5 + n_act :]
    cross_out, small_out, d_out = refs[:3]
    held, refs = refs[3 : 3 + n_act], refs[3 + n_act :]
    land_e, land_s, half_s, land_t = refs[:4]
    links = Links(n_dp, n_tensor, *refs[4:])
    loads = [links.local(src, dst) for src, dst in zip(acts, held)]
    links.barrier(True)
    copies_e = start_scatter(links, part_e, land_e)
    small_sent = [
        links.send(small.at[links.dp_peer(step)], land_s.at[step - 1], dp=links.dp_peer(step))
        for step in range(1, n_dp)
    ]
    for copy in loads:
        copy.wait()
    items = [
        (own, row_slot(ref, own.shape[0])) for own, ref in zip(held, act_out)
    ]
    gathered = DpGather(links, items)
    cross_sent = [
        links.send(cross.at[links.dp_peer(step)], cross_out.at[links.dp], dp=links.dp_peer(step))
        for step in range(1, n_dp)
    ]
    cross_kept = links.local(cross.at[links.dp], cross_out.at[links.dp])
    total = small[links.dp]
    for step, copy in enumerate(small_sent):
        copy.wait_recv()
        total = total + land_s[step]
    half_s[...] = total
    wide = [
        links.send(half_s, land_t.at[step - 1], tensor=links.tensor_peer(step))
        for step in range(1, n_tensor)
    ]
    grad = end_scatter(links, part_e, land_e, copies_e)
    d_out[...] = dres[...] + back_unit(resid[...], grad)
    for step, copy in enumerate(wide):
        copy.wait_recv()
        total = total + land_t[step]
    small_out[...] = total
    gathered.finish()
    for copy in cross_sent:
        copy.wait_recv()
    cross_kept.wait()
    links.finish()


def dot_nn(left, right):
    return jnp.dot(left, right, preferred_element_type=jnp.float32)


def dot_nt(left, right):
    return lax.dot_general(left, right, (((1,), (1,)), ((), ())), preferred_element_type=jnp.float32)


def dot_tn(left, right):
    return lax.dot_general(left, right, (((0,), (0,)), ((), ())), preferred_element_type=jnp.float32)


def turn(vectors, same, up, down, sign):
    width = vectors.shape[1]
    above = pltpu.roll(vectors, width - ROT // 2, 1)
    below = pltpu.roll(vectors, ROT // 2, 1)
    return vectors * same + sign * (above * up + below * down)


def head_scores(query, key, mask):
    scores = dot_nt(query, key) * HD ** (-0.5)
    scores = jnp.where(mask, scores, NEG_FILL)
    terms = jnp.exp(scores - jnp.max(scores, axis=-1, keepdims=True))
    return terms / jnp.sum(terms, axis=-1, keepdims=True)


def forward_math(
    unit, g1, b1, g2, b2, qkv_mat, qkv_vec, out_mat, fc_mat, fc_vec, proj_mat, mask, same, up, down,
    qkv_out, ctx_out, pre_out, act_out, part_out,
):
    bf16 = jnp.bfloat16
    wide = unit[...].astype(jnp.float32)
    normed_a = (wide * g1[...] + b1[...]).astype(bf16)
    normed_m = (wide * g2[...] + b2[...]).astype(bf16)
    projected = dot_nn(normed_a, qkv_mat[...]) + qkv_vec[...]
    part = ctx_out.shape[1]
    tables = (same[...], up[...], down[...])
    for which in range(3):
        block = projected[:, which * part : (which + 1) * part]
        if which < 2:
            block = turn(block, *tables, 1.0)
        qkv_out[:, which * part : (which + 1) * part] = block.astype(bf16)
    allowed = mask[...] > 0.0
    for head in range(part // HD):
        q, k, v = (
            qkv_out[:, which * part + head * HD : which * part + (head + 1) * HD]
            for which in range(3)
        )
        probs = head_scores(q, k, allowed).astype(bf16)
        ctx_out[:, head * HD : (head + 1) * HD] = dot_nn(probs, v).astype(bf16)
    hidden = dot_nn(normed_m, fc_mat[...]) + fc_vec[...]
    pre_out[...] = hidden
    act_out[...] = gelu_exact(hidden).astype(bf16)
    part_out[...] = (dot_nn(ctx_out[...], out_mat[...]) + dot_nn(act_out[...], proj_mat[...])).astype(
        bf16
    )


def backward_math(
    unit, g1, g2, qkv_mat, out_mat, fc_mat, proj_mat, mask, same, up, down, d_rows, qkv, ctx, pre,
    dqkv_out, du_out, part_out, sums_out, d_ctx,
):
    bf16, f32 = jnp.bfloat16, jnp.float32
    d_ctx[...] = dot_nt(d_rows[...], out_mat[...]).astype(bf16)
    du_out[...] = (dot_nt(d_rows[...], proj_mat[...]) * gelu_slope(pre[...])).astype(bf16)
    part = ctx.shape[1]
    allowed = mask[...] > 0.0
    pieces = [[], [], []]
    for head in range(part // HD):
        here = slice(head * HD, (head + 1) * HD)
        q, k, v = (
            qkv[:, which * part + head * HD : which * part + (head + 1) * HD] for which in range(3)
        )
        dc = d_ctx[:, here]
        probs = head_scores(q, k, allowed)
        delta = jnp.sum(dc.astype(f32) * ctx[:, here].astype(f32), axis=-1, keepdims=True)
        d_scaled = (probs * (dot_nt(dc, v) - delta) * HD ** (-0.5)).astype(bf16)
        pieces[0].append(dot_nn(d_scaled, k))
        pieces[1].append(dot_tn(d_scaled, q))
        pieces[2].append(dot_tn(probs.astype(bf16), dc))
    tables = (same[...], up[...], down[...])
    for which in range(3):
        block = jnp.concatenate(pieces[which], axis=1)
        if which < 2:
            block = turn(block, *tables, -1.0)
        dqkv_out[:, which * part : (which + 1) * part] = block.astype(bf16)
    d_a = dot_nt(dqkv_out[...], qkv_mat[...])
    d_m = dot_nt(du_out[...], fc_mat[...])
    wide = unit[...].astype(f32)
    sums_out[0:1] = jnp.sum(d_a * wide, axis=0, keepdims=True)
    sums_out[1:2] = jnp.sum(d_a, axis=0, keepdims=True)
    sums_out[2:3] = jnp.sum(d_m * wide, axis=0, keepdims=True)
    sums_out[3:4] = jnp.sum(d_m, axis=0, keepdims=True)
    part_out[...] = (d_a * g1[...] + d_m * g2[...]).astype(bf16)


def weight_grads_math(layers, cross, *refs):
    vectors, refs = refs[0], refs[1:]
    acts, (qkv_g, out_g, fc_g, proj_g, qkv_s, fc_s) = refs[: 4 * layers], refs[4 * layers :]
    bf16, f32 = jnp.bfloat16, jnp.float32
    width = cross.shape[-1]
    for layer in range(layers):
        context, act, dqkv, d_pre = acts[4 * layer : 4 * layer + 4]
        unit = cross[:, layer, 0].reshape(-1, width).astype(f32)
        d_t = cross[:, layer, 1].reshape(-1, width)
        g1, b1, g2, b2 = (vectors[layer, row : row + 1] for row in range(4))
        a_t = (unit * g1 + b1).astype(bf16)
        m_t = (unit * g2 + b2).astype(bf16)
        qkv_g[layer] = dot_tn(a_t, dqkv[...])
        fc_g[layer] = dot_tn(m_t, d_pre[...])
        out_g[layer] = jnp.transpose(dot_tn(d_t, context[...]))
        proj_g[layer] = jnp.transpose(dot_tn(d_t, act[...]))
        qkv_s[layer : layer + 1] = jnp.sum(dqkv[...].astype(f32), axis=0, keepdims=True)
        fc_s[layer : layer + 1] = jnp.sum(d_pre[...].astype(f32), axis=0, keepdims=True)


def plain(kernel, name, outs, scratch, args):
    return pl.pallas_call(
        kernel,
        out_shape=outs,
        in_specs=[VMEM] * len(args),
        out_specs=(VMEM,) * len(outs),
        scratch_shapes=scratch,
        name=name,
        compiler_params=pltpu.CompilerParams(vmem_limit_bytes=40 << 20),
    )(*args)


def call(kernel, name, collective, outs, out_specs, in_specs, scratch, args):
    return pl.pallas_call(
        kernel,
        out_shape=outs,
        in_specs=in_specs,
        out_specs=out_specs,
        scratch_shapes=scratch + scratch_sems(),
        name=name,
        compiler_params=pltpu.CompilerParams(
            collective_id=collective, has_side_effects=True, vmem_limit_bytes=40 << 20
        ),
    )(*args)


def shaped(shape, dtype):
    return jax.ShapeDtypeStruct(tuple(shape), dtype)


def pack_rows(parts):
    flat = jnp.concatenate([part.reshape(-1) for part in parts])
    padded = -(-flat.shape[0] // 1024) * 1024
    return jnp.pad(flat, (0, padded - flat.shape[0])).reshape(-1, 128)


def per_device(
    x_in,
    seq_lengths,
    ln1_gain,
    ln1_bias,
    ln2_gain,
    ln2_bias,
    res_bias,
    w_qkv,
    b_qkv,
    w_out,
    w_fc,
    b_fc,
    w_proj,
    grad_out,
):
    n_tensor, n_dp = lax.axis_size("tensor"), lax.axis_size("dp")
    my_tensor = lax.axis_index("tensor")
    bf16, f32 = jnp.bfloat16, jnp.float32
    my_rows, width = x_in.shape
    group_rows = my_rows * n_tensor
    total_rows = group_rows * n_dp
    layer_count = w_qkv.shape[0]
    heads_here = w_qkv.shape[3] // HD
    dp_width = width // n_dp
    vec_width = dp_width // n_tensor

    columns_ok = dp_width % 128 == 0
    shards = (w_qkv.reshape(layer_count, dp_width, -1), w_out, w_fc, w_proj)
    axes = (0, 1 if columns_ok else None, 0, 1 if columns_ok else None)
    gathered = []
    for shard, axis in zip(shards, axes):
        shape = list(shard.shape[1:])
        if axis is None:
            shape = [n_dp] + shape
        else:
            shape[axis] *= n_dp
        gathered.append(shaped(shape, bf16))
    smalls = (
        jnp.stack([ln1_gain, ln1_bias, ln2_gain, ln2_bias, res_bias]),
        b_qkv,
        b_fc,
    )
    packed = pack_rows(smalls)
    unit_shape, d_shape = shaped((group_rows, width), bf16), shaped(x_in.shape, f32)
    own_rows = pltpu.VMEM((my_rows, width), bf16)
    land = pltpu.VMEM((n_tensor - 1, my_rows, width), bf16)
    held = [pltpu.VMEM(shard.shape[1:], bf16) for shard in shards]
    entry = call(
        functools.partial(entry_kernel, n_dp, n_tensor, axes),
        "entry",
        0,
        tuple(gathered)
        + (shaped((n_tensor, n_dp) + packed.shape, f32), unit_shape, unit_shape),
        (ANY,) * 4 + (VMEM,) * 3,
        [ANY] * 4 + [VMEM] * 3,
        held + [own_rows] * 2,
        shards + (packed, x_in, grad_out),
    )
    small_all, unit_full, d_rows = entry[4:]

    def in_columns(matrix):
        if matrix.ndim == 2:
            return matrix
        return jnp.transpose(matrix, (1, 0, 2)).reshape(-1, width)

    weights = [tuple(in_columns(matrix) for matrix in entry[:4])]
    small_all = small_all.reshape(n_tensor, n_dp, -1)
    n_gain = smalls[0].size
    vectors = jnp.transpose(
        small_all[:, :, :n_gain].reshape(n_tensor, n_dp, 5, layer_count, vec_width),
        (2, 3, 1, 0, 4),
    ).reshape(5, layer_count, width)
    gain_one, bias_one, gain_two, bias_two, out_bias = vectors
    mine = lax.dynamic_index_in_dim(small_all, my_tensor, 0, keepdims=False)
    qkv_vecs = jnp.transpose(
        mine[:, n_gain : n_gain + b_qkv.size].reshape((n_dp,) + b_qkv.shape), (1, 2, 0, 3)
    ).reshape(layer_count, 1, -1)
    fc_vecs = jnp.transpose(
        mine[:, n_gain + b_qkv.size : n_gain + b_qkv.size + b_fc.size].reshape(
            (n_dp,) + b_fc.shape
        ),
        (1, 0, 2),
    ).reshape(layer_count, 1, -1)

    seq_ids, positions, row_ids = group_layout(seq_lengths[0], group_rows)
    cos_tab, sin_tab = rotary_tables(positions)
    flat = jnp.zeros((group_rows, HD - ROT), f32)
    none = jnp.zeros_like(sin_tab)
    same = jnp.tile(jnp.concatenate([cos_tab, cos_tab, flat + 1.0], axis=1), (1, heads_here))
    up = jnp.tile(jnp.concatenate([-sin_tab, none, flat], axis=1), (1, heads_here))
    down = jnp.tile(jnp.concatenate([none, sin_tab, flat], axis=1), (1, heads_here))
    mask = (
        (seq_ids[:, None] == seq_ids[None, :]) & (row_ids[None, :] <= row_ids[:, None])
    ).astype(f32)
    tables = (mask, same, up, down)
    part_width = heads_here * HD
    resid = x_in
    saved = []
    for layer in range(layer_count):
        qkv_mat, out_mat, fc_mat, proj_mat = weights[layer]
        gains = tuple(
            vector[layer][None] for vector in (gain_one, bias_one, gain_two, bias_two)
        )
        qkv_flat, flat_context, hidden_pre, activated, partial = plain(
            forward_math,
            f"math_forward{layer}",
            (
                shaped((group_rows, 3 * part_width), bf16),
                shaped((group_rows, part_width), bf16),
                shaped((group_rows, fc_mat.shape[1]), f32),
                shaped((group_rows, fc_mat.shape[1]), bf16),
                unit_shape,
            ),
            [],
            (unit_full,)
            + gains
            + (qkv_mat, qkv_vecs[layer], out_mat, fc_mat, fc_vecs[layer], proj_mat)
            + tables,
        )
        saved.append((resid, unit_full, qkv_flat, flat_context, hidden_pre, activated, gains))
        if layer + 1 < layer_count:
            stepped = call(
                functools.partial(forward_kernel, n_dp, n_tensor, axes, layer),
                f"forward{layer}",
                1 + layer,
                (d_shape, unit_shape) + tuple(gathered),
                (VMEM,) * 2 + (ANY,) * 4,
                [VMEM] * 3 + [ANY] * 4,
                [land, own_rows] + held,
                (partial, resid, out_bias[layer][None]) + shards,
            )
            resid, unit_full = stepped[:2]
            weights.append(tuple(in_columns(matrix) for matrix in stepped[2:]))
    d_resid = grad_out
    acts, cross, sums = [None] * layer_count, [None] * layer_count, [None] * layer_count
    all_acts = [None] * layer_count
    for layer in reversed(range(layer_count)):
        layer_input, unit_full, qkv_flat, flat_context, hidden_pre, activated, gains = saved[layer]
        qkv_mat, out_mat, fc_mat, proj_mat = weights[layer]
        flat_dqkv, d_pre_b, part_e, vector_sums = plain(
            backward_math,
            f"math_backward{layer}",
            (
                shaped(qkv_flat.shape, bf16),
                shaped(activated.shape, bf16),
                unit_shape,
                shaped((4, width), f32),
            ),
            [pltpu.VMEM((group_rows, part_width), bf16)],
            (unit_full, gains[0], gains[2], qkv_mat, out_mat, fc_mat, proj_mat)
            + tables
            + (d_rows, qkv_flat, flat_context, hidden_pre),
        )
        sums[layer] = jnp.concatenate([vector_sums, jnp.sum(d_resid, axis=0)[None]])
        acts[layer] = (flat_context, activated, flat_dqkv, d_pre_b)
        cross[layer] = jnp.stack([unit_full, d_rows]).reshape(2, group_rows, n_dp, dp_width)
        if layer > 0:
            last = layer + 1 == layer_count
            n_act = len(acts[layer])
            stepped = call(
                functools.partial(backward_kernel, n_dp, n_tensor, n_act, last),
                f"backward{layer}",
                layer_count + layer,
                tuple(shaped((total_rows, array.shape[1]), bf16) for array in acts[layer])
                + (d_shape, unit_shape)
                + ((d_shape,) if last else ()),
                (ANY,) * n_act + (VMEM,) * (3 if last else 2),
                [ANY] * n_act + [VMEM] * (5 if last else 3),
                [pltpu.VMEM(array.shape, bf16) for array in acts[layer]]
                + [land, own_rows]
                + ([land] if last else []),
                acts[layer]
                + (part_e, layer_input, d_resid)
                + ((partial, out_bias[layer][None]) if last else ()),
            )
            all_acts[layer] = stepped[:n_act]
            d_resid, d_rows = stepped[n_act : n_act + 2]
            if last:
                y_out = stepped[n_act + 2]
    flat_acts = acts[0]
    n_act = len(flat_acts)
    cross_in = jnp.transpose(jnp.stack(cross), (3, 0, 1, 2, 4))
    stacked = jnp.stack(sums).reshape(-1, width)
    n_sums = stacked.shape[0]
    padded = -(-n_sums // 8) * 8
    small_in = jnp.transpose(
        jnp.pad(stacked, ((0, padded - n_sums), (0, 0))).reshape(padded, n_dp, dp_width), (1, 0, 2)
    )
    small_block = (padded, dp_width)
    results = call(
        functools.partial(exit_kernel, n_dp, n_tensor, n_act),
        "exit",
        2 * layer_count,
        tuple(shaped((total_rows, array.shape[1]), bf16) for array in flat_acts)
        + (shaped(cross_in.shape, bf16), shaped(small_block, f32), shaped(x_in.shape, f32)),
        (ANY,) * n_act + (VMEM,) * 3,
        [ANY] * n_act + [VMEM] * 5,
        [pltpu.VMEM(array.shape, bf16) for array in flat_acts]
        + [
            land,
            pltpu.VMEM((n_dp - 1,) + small_block, f32),
            pltpu.VMEM(small_block, f32),
            pltpu.VMEM((n_tensor - 1,) + small_block, f32),
        ],
        tuple(flat_acts) + (cross_in, small_in, part_e, layer_input, d_resid),
    )
    all_acts[0], (cross_all, small_sum, grad_x) = results[:n_act], results[n_act:]
    my_dp = lax.axis_index("dp")
    in_vmem = total_rows * sum(array.shape[1] for array in acts[0]) * 2 * layer_count <= 16 << 20
    if in_vmem and columns_ok:
        vectors = jnp.transpose(jnp.stack([gain_one, bias_one, gain_two, bias_two]), (1, 0, 2))
        vectors = lax.dynamic_slice_in_dim(vectors, my_dp * dp_width, dp_width, axis=2)
        flat_qkv, out_g, fc_g, proj_g, qkv_s, fc_s = plain(
            functools.partial(weight_grads_math, layer_count),
            "math_grads",
            (
                shaped((layer_count, dp_width, 3 * part_width), f32),
                shaped(w_out.shape, f32),
                shaped(w_fc.shape, f32),
                shaped(w_proj.shape, f32),
                shaped((layer_count, 3 * part_width), f32),
                shaped((layer_count, w_fc.shape[2]), f32),
            ),
            [],
            (cross_all, vectors) + tuple(array for group in all_acts for array in group),
        )
        stacked_grads = (
            flat_qkv.reshape(w_qkv.shape),
            lax.dynamic_slice_in_dim(
                qkv_s.reshape(layer_count, 3, -1), my_dp * b_qkv.shape[2], b_qkv.shape[2], axis=2
            ),
            out_g,
            fc_g,
            lax.dynamic_slice_in_dim(fc_s, my_dp * b_fc.shape[1], b_fc.shape[1], axis=1),
            proj_g,
        )
    else:
        over_tokens = (((0,), (0,)), ((), ()))
        grads = [[] for _ in range(6)]
        for layer in range(layer_count):
            context_t, act_t, dqkv_t, d_pre_t = all_acts[layer]
            unit_t = cross_all[:, layer, 0].reshape(total_rows, dp_width).astype(f32)
            d_t = cross_all[:, layer, 1].reshape(total_rows, dp_width)

            def here(vector):
                return lax.dynamic_slice_in_dim(vector[layer], my_dp * dp_width, dp_width)

            a_t = (unit_t * here(gain_one) + here(bias_one)).astype(bf16)
            m_t = (unit_t * here(gain_two) + here(bias_two)).astype(bf16)

            def contract(left, right):
                return lax.dot_general(left, right, over_tokens, preferred_element_type=f32)

            qkv_sums = jnp.sum(dqkv_t.astype(f32), axis=0).reshape(3, -1)
            fc_sums = jnp.sum(d_pre_t.astype(f32), axis=0)
            grads[0].append(contract(a_t, dqkv_t).reshape(w_qkv.shape[1:]))
            grads[1].append(
                lax.dynamic_slice_in_dim(qkv_sums, my_dp * b_qkv.shape[2], b_qkv.shape[2], axis=1)
            )
            grads[2].append(contract(context_t, d_t))
            grads[3].append(contract(m_t, d_pre_t))
            grads[4].append(lax.dynamic_slice_in_dim(fc_sums, my_dp * b_fc.shape[1], b_fc.shape[1]))
            grads[5].append(contract(act_t, d_t))
        stacked_grads = tuple(jnp.stack(group) for group in grads)
    vector_grads = lax.dynamic_slice_in_dim(
        small_sum[:n_sums].reshape(layer_count, 5, dp_width), my_tensor * vec_width, vec_width, axis=2
    )
    return (
        y_out,
        grad_x,
        vector_grads[:, 0],
        vector_grads[:, 1],
        vector_grads[:, 2],
        vector_grads[:, 3],
        vector_grads[:, 4],
    ) + stacked_grads


def solution(mesh):
    in_specs = (
        P(("dp", "tensor"), None),
        P("dp", None),
        P(None, ("dp", "tensor")),
        P(None, ("dp", "tensor")),
        P(None, ("dp", "tensor")),
        P(None, ("dp", "tensor")),
        P(None, ("dp", "tensor")),
        P(None, "dp", None, "tensor"),
        P(None, None, ("tensor", "dp")),
        P(None, "tensor", "dp"),
        P(None, "dp", "tensor"),
        P(None, ("tensor", "dp")),
        P(None, "tensor", "dp"),
        P(("dp", "tensor"), None),
    )
    out_specs = (
        P(("dp", "tensor"), None),
        P(("dp", "tensor"), None),
        P(None, ("dp", "tensor")),
        P(None, ("dp", "tensor")),
        P(None, ("dp", "tensor")),
        P(None, ("dp", "tensor")),
        P(None, ("dp", "tensor")),
        P(None, "dp", None, "tensor"),
        P(None, None, ("tensor", "dp")),
        P(None, "tensor", "dp"),
        P(None, "dp", "tensor"),
        P(None, ("tensor", "dp")),
        P(None, "tensor", "dp"),
    )
    return jax.shard_map(
        per_device, mesh=mesh, in_specs=in_specs, out_specs=out_specs, check_vma=False
    )
```
